256 devices in a mesh: span: 4 (over x), wrap: 16 (over y_hi, z), blade: 4 (over y_lo, core).
Axes of the slice: x: 4, y: 4 (y_hi: 2, y_lo: 2; y = y_hi * 2 + y_lo), z: 8, core: 2. Of those that a mesh axis runs over, the one named last changes fastest.
Arguments:
- state: float32 [4, 5, 16, 1024, 128], P('blade', None, 'span', 'wrap'), may hold values from -6 to 6
- state_old: float32 [4, 5, 16, 1024, 128], P('blade', None, 'span', 'wrap'), may hold values from -6 to 6
- wrap_rate: float32 [4, 5, 16, 128], P('blade', None, 'span'), may hold values from 0.5 to 64
- span_rate: float32 [4, 5, 1024, 128], P('blade', None, 'wrap'), may hold values from 0.5 to 64
- blank: int32 [4, 16, 1024, 64], P('blade', 'span', 'wrap'), may hold values from 0 to 2
- section: int32 [4, 16, 1024], P('blade', 'span', 'wrap'), may hold values from 0 to 639
Outputs:
- updated: float32 [4, 5, 16, 1024, 128], P('blade', None, 'span', 'wrap')
- loads: float32 [4, 3, 640], P('blade', None, ('span', 'wrap'))
The draws below stay inside these ranges and needn't reach their ends.
Inputs may be any that keep to these rules, and one draw needn't show every extreme that they name: `blank`: 0 marks an ordinary point, 1 a fringe point served by the preceding blade, 2 one served by the following blade, blades closed cyclically.
All inputs are finite; a program needn't handle non-finite values.
Results may differ from the reference program's by a relative error of at most 0.0003.
Values sent between devices are 32-bit elements; how exact they have to be, the bound alone decides.
A program may use at most 128 MiB of HBM per device.

```python
import math
import jax
import jax.numpy as jnp
from jax import lax

NN = 128
NF = 64
SECTIONS = 640
NS = 16
NW = 1024
BLADES = 4


def place_ends(array, own_key, least, largest):
    shape = array.shape
    spot = [jax.random.randint(jax.random.fold_in(own_key, axis), (), 0, shape[axis]) for axis in range(len(shape))]
    array = array.at[tuple(spot)].set(least)
    longest = shape.index(max(shape))
    spot[longest] = (spot[longest] + 1) % shape[longest]
    return array.at[tuple(spot)].set(largest)


def shard_levels(own_key, dims, shards, low, largest):
    loudness = 1.0
    for dim, parts in shards:
        heights = jax.random.uniform(jax.random.fold_in(jax.random.fold_in(own_key, 6), dim), (parts,), jnp.float32, low / len(shards), largest / len(shards))
        loudness = loudness * jnp.repeat(jnp.exp(heights), dims[dim] // parts).reshape((-1,) + (1,) * (len(dims) - 1 - dim))
    return loudness


def bell_draw(own_key, shape, deviation, most, cuts=(), kind=jnp.bfloat16):
    loudness = shard_levels(own_key, shape, cuts, -0.22, 0.18) if cuts else 1.0
    values = jax.random.normal(own_key, shape, jnp.float32) * deviation * loudness
    return jnp.minimum(jnp.maximum(values, -most), most).astype(kind)


def setup_inputs(seed: int = 0) -> dict:
    key_of = jax.random.split(jax.random.key(seed), 7)
    return {
        "state": bell_draw(key_of[0], (BLADES, 5, NS, NW, NN), 1.0, 6.0, ((0, 4), (2, 4), (3, 16)), jnp.float32),
        "state_old": bell_draw(key_of[1], (BLADES, 5, NS, NW, NN), 1.0, 6.0, ((0, 4), (2, 4), (3, 16)), jnp.float32),
        "wrap_rate": jnp.clip(jnp.exp(math.log(64.0) - 4.8520303 * jax.random.uniform(key_of[2], (BLADES, 5, NS, NN), jnp.float32) ** shard_levels(key_of[2], (BLADES, 5, NS, NN), ((0, 4), (2, 4)), -0.2, 0.2)), 0.5, 64.0),
        "span_rate": jnp.clip(jnp.exp(math.log(64.0) - 4.8520303 * jax.random.uniform(key_of[3], (BLADES, 5, NW, NN), jnp.float32) ** shard_levels(key_of[3], (BLADES, 5, NW, NN), ((0, 4), (2, 16)), -0.2, 0.2)), 0.5, 64.0),
        "blank": place_ends(jax.random.randint(key_of[4], (BLADES, NS, NW, NF), 0, 3), jax.random.fold_in(key_of[4], 1), 0, 2).astype(jnp.int32),
        "section": place_ends(jax.random.randint(key_of[5], (BLADES, NS, NW), 0, SECTIONS), jax.random.fold_in(key_of[5], 1), 0, SECTIONS - 1).astype(jnp.int32),
    }


def shifted(values, offset, axis_at):
    length_at = values.shape[axis_at]
    widths = [(0, 0)] * values.ndim
    widths[axis_at] = (2, 2)
    padded = jnp.pad(values, widths)
    return lax.slice_in_dim(padded, 2 + offset, 2 + offset + length_at, axis=axis_at)


def fourth(getter):
    return getter(2) - 4.0 * getter(1) + 6.0 * getter(0) - 4.0 * getter(-1) + getter(-2)


def residual_rhs(field, state_old, chord_get, span_get, normal_get):
    return ((state_old - field) - 0.5 * (chord_get(1) - chord_get(-1)) - 0.5 * (span_get(1) - span_get(-1))
            + 0.25 * (normal_get(1) - 2.0 * field + normal_get(-1)) - 0.05 * (fourth(chord_get) + fourth(span_get)))


def chord_symbol(frequency, total):
    cosine = jnp.cos(2.0 * jnp.pi * frequency.astype(jnp.float32) / total)
    differ = 2.0 - 2.0 * cosine
    return differ + 0.5 * differ * differ


def factors(rates, total):
    centre = 1.0 + 5.0 * rates
    first_band = -3.0 * rates
    second_band = 0.5 * rates

    def advance(carry, position):
        diag_one, diag_two, lower_prev = carry
        low_two = jnp.where(position >= 2, second_band / diag_two, 0.0)
        low_one = jnp.where(position >= 1, (first_band - low_two * diag_two * lower_prev) / diag_one, 0.0)
        pivot = centre - low_one * low_one * diag_one - low_two * low_two * diag_two
        return (pivot, diag_one, low_one), (low_one, low_two, pivot)

    unit_diag = jnp.ones_like(rates)
    zero_band = jnp.zeros_like(rates)
    final_state, stacked = lax.scan(advance, (unit_diag, unit_diag, zero_band), jnp.arange(total, dtype=jnp.int32))
    return stacked


def recurrence(carry, item):
    prev_one, prev_two = carry
    source, coeff_one, coeff_two = item
    value_now = source - coeff_one * prev_one - coeff_two * prev_two
    return (value_now, prev_one), value_now


def span_solve(data, rates):
    total = data.shape[0]
    lower_one, lower_two, pivots = factors(rates, total)
    zero_state = jnp.zeros_like(rates)
    carry_out, ahead = lax.scan(recurrence, (zero_state, zero_state), (data, lower_one, lower_two))
    scaled = ahead / pivots
    upper_one = jnp.concatenate([lower_one[1:], zero_state[None]], 0)
    upper_two = jnp.concatenate([lower_two[2:], zero_state[None], zero_state[None]], 0)
    carry_back, result = lax.scan(recurrence, (zero_state, zero_state), (scaled, upper_one, upper_two), reverse=True)
    return result


def reference(state, state_old, wrap_rate, span_rate, blank, section):
    outer = state[..., NN - NF:]
    below = jnp.roll(outer, 1, axis=0)
    above = jnp.roll(outer, -1, axis=0)
    marks = blank[:, None]
    fringe = jnp.where(marks == 1, below, jnp.where(marks == 2, above, outer))
    field = jnp.concatenate([state[..., :NN - NF], fringe], axis=4)

    def chord_get(offset):
        return jnp.roll(field, -offset, axis=3)

    def span_get(offset):
        return shifted(field, offset, 2)

    def normal_get(offset):
        return shifted(field, offset, 4)

    rhs = residual_rhs(field, state_old, chord_get, span_get, normal_get)
    frequency = jnp.arange(NW, dtype=jnp.int32)
    symbol = chord_symbol(frequency, NW)
    eigen_value = 1.0 + wrap_rate[:, :, :, None, :] * symbol[None, None, None, :, None]
    spectrum = jnp.fft.fft(rhs, axis=3)
    solved = jnp.real(jnp.fft.ifft(spectrum / eigen_value, axis=3)).astype(rhs.dtype)
    span_first = jnp.moveaxis(solved, 2, 0)
    update = span_solve(span_first, span_rate)
    updated = field + jnp.moveaxis(update, 0, 2)
    stress = updated[:, 1:4, :, :, 1] - updated[:, 1:4, :, :, 0]
    blades = stress.shape[0]
    nodes = stress.reshape(blades, 3, NS * NW)
    picks = (section.reshape(blades, NS * NW)[:, :, None] == jnp.arange(SECTIONS, dtype=jnp.int32)[None, None, :]).astype(stress.dtype)
    loads = jnp.einsum("bkn,bns->bks", nodes, picks, precision=lax.Precision.HIGHEST)
    return (updated, loads)
```

```python
import jax
import jax.numpy as jnp
from jax import lax
from jax.experimental import pallas as pl
from jax.experimental.pallas import tpu as pltpu
from jax.sharding import PartitionSpec as P

MESH = pl.DeviceIdType.MESH
SECTIONS = 640
V, S, W, N = 5, 4, 64, 128
H = W // 2
GROUP = 4
SPANS, WRAPS, BLADES = 4, 16, 4
LEVELS = 6


def var_of(slot):
    return jnp.where(slot < 3, slot + 1, jnp.where(slot == 3, 0, 4))


def var_static(slot):
    return (1, 2, 3, 0, 4)[slot]


def line_roots(r):
    ri = 1.0 / r
    y = 6.0 + ri + jnp.sqrt(ri * (12.0 + ri))
    q = 2.0 / ((y - 2.0) + jnp.sqrt(y * (y - 4.0)))
    p = 6.0 * q / (1.0 + q)
    return p, q


def square(m):
    a, b, c, d = m
    bc = b * c
    tr = a + d
    return a * a + bc, b * tr, c * tr, d * d + bc


def kernel(
    state, old, wrate, srate, blank, section,
    out, loads,
    st, so, wr, sr, bl, mk, sec, pk, fb, fa, fl, hlo, hhi, cslo, cshi, crlo, crhi, fr,
    ga, gd, ub, ud, cf, r8, tm, ms, m1, gs, m2, cc, xb, l1t, l2t, rdt, alt, bet,
    ysend, yrecv, asend, arecv, xsend, xrecv, ob, la, lra, ld, lrb,
    in_s, st_s, out_s, fs, fq, hs, hq, cs, cq, r1s, r1q, r2s, r2q, ys, yq, as_, aq, xs, xq,
    las, laq, lbs, lbq,
):
    span = lax.axis_index("span")
    wrap = lax.axis_index("wrap")
    blade = lax.axis_index("blade")
    place = wrap % GROUP
    group = wrap // GROUP
    groups = WRAPS // GROUP

    barrier = pltpu.get_barrier_semaphore()
    for d in (1, BLADES - 1):
        pl.semaphore_signal(barrier, inc=1, device_id={"blade": (blade + d) % BLADES}, device_id_type=MESH)
    for d in range(1, SPANS):
        pl.semaphore_signal(barrier, inc=1, device_id={"span": (span + d) % SPANS}, device_id_type=MESH)
    for d in range(1, WRAPS):
        pl.semaphore_signal(barrier, inc=1, device_id={"wrap": (wrap + d) % WRAPS}, device_id_type=MESH)

    loads_in = []
    for i in range(V):
        loads_in.append(pltpu.make_async_copy(state.at[0, var_static(i)], st.at[i], st_s.at[i]))
    loads_in.append(pltpu.make_async_copy(wrate.at[0], wr, in_s.at[0]))
    loads_in.append(pltpu.make_async_copy(blank.at[0], bl, in_s.at[1]))
    for i in range(V):
        loads_in.append(pltpu.make_async_copy(srate.at[0, var_static(i)], sr.at[i], in_s.at[2 + i]))
    for i in range(V):
        loads_in.append(pltpu.make_async_copy(old.at[0, var_static(i)], so.at[i], in_s.at[7 + i]))
    loads_in.append(pltpu.make_async_copy(section.at[0], sec, in_s.at[12]))
    for copy in loads_in:
        copy.start()

    lane_h = lax.broadcasted_iota(jnp.int32, (H, N), 1)
    lane_w = lax.broadcasted_iota(jnp.int32, (W, N), 1)
    row_w = lax.broadcasted_iota(jnp.int32, (W, N), 0)
    row_8 = lax.broadcasted_iota(jnp.int32, (8, N), 0)

    for i in range(V):
        loads_in[i].wait()

    def pack(i, c):
        for s in range(S):
            low = st[i, s, 0:H, :]
            high = st[i, s, H:W, :]
            pk[i, s] = jnp.where(lane_h < N // 2, pltpu.roll(low, N // 2, 1), high)
        return c

    lax.fori_loop(0, V, pack, 0)

    pl.semaphore_wait(barrier, 2 + SPANS - 1 + WRAPS - 1)

    def fringe_up(i):
        return pltpu.make_async_remote_copy(
            src_ref=pk.at[i], dst_ref=fb.at[i], send_sem=fs.at[0, i], recv_sem=fq.at[0, i],
            device_id={"blade": (blade + 1) % BLADES}, device_id_type=MESH)

    def fringe_down(i):
        return pltpu.make_async_remote_copy(
            src_ref=pk.at[i], dst_ref=fa.at[i], send_sem=fs.at[1, i], recv_sem=fq.at[1, i],
            device_id={"blade": (blade + BLADES - 1) % BLADES}, device_id_type=MESH)

    def fringe_send(i, c):
        fringe_up(i).start()
        fringe_down(i).start()
        return c

    lax.fori_loop(0, V, fringe_send, 0)

    for copy in loads_in[V:]:
        copy.wait()

    for s in range(S):
        mk[s] = jnp.concatenate([bl[s, 0:H, :], bl[s, H:W, :]], axis=-1)

    def chord_tables(idx, c):
        i = idx // S
        s = idx % S
        r = jnp.broadcast_to(wr[var_of(i), pl.ds(s, 1), :], (8, N))
        p, q = line_roots(r)
        g0 = (1.0 + q) * (2.0 * q) / (r * (1.0 - q) * (1.0 + q - p) * (1.0 + q + p))
        ratio = p / (1.0 + q)
        g1 = g0 * ratio
        rows = []
        pk_, qk_ = [p], [q]
        for k in range(LEVELS - 1):
            pk_.append(pk_[-1] * pk_[-1] - 2.0 * qk_[-1])
            qk_.append(qk_[-1] * qk_[-1])
        rows = pk_ + qk_ + [g0, -g1 * q, g1, -q * g0]

        def pick(values):
            tile = values[0]
            for n in range(1, 8):
                tile = jnp.where(row_8 == n, values[n], tile)
            return tile

        cf[i, s, 0:8, :] = pick(rows[0:8])
        cf[i, s, 8:16, :] = pick(rows[8:16])
        g = [g0, g1]
        for n in range(2, 17):
            g.append(p * g[-1] - q * g[-2])
        zero = jnp.zeros_like(p)
        u = [zero, zero + 1.0]
        for n in range(2, 17):
            u.append(p * u[-1] - q * u[-2])
        p3, q3 = pk_[3], qk_[3]

        def ascend(table, first, second):
            table[i, s, 0:8, :] = first
            table[i, s, 8:16, :] = second
            before, now = first, second
            for t in range(2, 9):
                before, now = now, p3 * now - q3 * before
                table[i, s, 8 * t : 8 * t + 8, :] = now

        def descend(table, last, first, second):
            table[i, s, 64:72, :] = last
            table[i, s, 56:64, :] = first
            table[i, s, 48:56, :] = second
            before, now = first, second
            for t in range(5, -1, -1):
                before, now = now, p3 * now - q3 * before
                table[i, s, 8 * t : 8 * t + 8, :] = now

        ascend(ga, pick(g[0:8]), pick(g[8:16]))
        descend(gd, jnp.where(row_8 == 0, g0, 0.0), pick(g[8:0:-1]), pick(g[16:8:-1]))
        ascend(ub, pick(u[0:8]), pick(u[8:16]))
        descend(ud, zero, pick(u[8:0:-1]), pick(u[16:8:-1]))
        return c

    lax.fori_loop(0, V * S, chord_tables, 0)

    def transfers(i, c):
        rate = wr[var_of(i)]
        r8[0:S, :] = rate
        r8[S : 2 * S, :] = rate
        p, q = line_roots(r8[...])
        m = (p, -q, jnp.ones_like(p), jnp.zeros_like(p))
        for k in range(LEVELS):
            m = square(m)
        for k in range(4):
            tm[i, k] = m[k]
        m = square(square(m))
        for k in range(4):
            tm[i, 4 + k] = m[k]
        return c

    lax.fori_loop(0, V, transfers, 0)

    def span_tables(idx, c):
        i = idx // 8
        rows = pl.ds(pl.multiple_of((idx % 8) * 8, 8), 8)
        r = sr[i, rows, :]
        centre = 1.0 + 5.0 * r
        first = -3.0 * r
        second = 0.5 * r
        zero = jnp.zeros_like(r)
        one_l, two_l, rd = [zero], [zero], [1.0 / centre]
        for j in range(1, 10):
            two = second * rd[j - 2] if j >= 2 else zero
            two_l.append(two)
            if j == 9:
                break
            top = first - second * one_l[j - 1]
            one = top * rd[j - 1]
            one_l.append(one)
            if j < 8:
                rd.append(1.0 / (centre - one * top - two * second))
        for j in range(9):
            l1t[i, j, rows, :] = one_l[j]
        for j in range(10):
            l2t[i, j, rows, :] = two_l[j]
        for j in range(8):
            rdt[i, j, rows, :] = rd[j]
        alpha = 1.0 - two_l[9] * two_l[8]
        beta = one_l[8] - two_l[9] * one_l[7]
        det = 1.0 / ((alpha - beta) * (alpha + beta))
        alt[i, rows, :] = alpha * det
        bet[i, rows, :] = beta * det
        return c

    lax.fori_loop(0, V * 8, span_tables, 0)

    def halo_up(i):
        return pltpu.make_async_remote_copy(
            src_ref=fl.at[i, 2:4, 8 : 8 + W, :], dst_ref=hlo.at[i], send_sem=hs.at[0, i], recv_sem=hq.at[0, i],
            device_id={"span": (span + 1) % SPANS}, device_id_type=MESH)

    def halo_down(i):
        return pltpu.make_async_remote_copy(
            src_ref=fl.at[i, 0:2, 8 : 8 + W, :], dst_ref=hhi.at[i], send_sem=hs.at[1, i], recv_sem=hq.at[1, i],
            device_id={"span": (span + SPANS - 1) % SPANS}, device_id_type=MESH)

    def chord_up(i):
        return pltpu.make_async_remote_copy(
            src_ref=cshi.at[i], dst_ref=crlo.at[i], send_sem=cs.at[0, i], recv_sem=cq.at[0, i],
            device_id={"wrap": (wrap + 1) % WRAPS}, device_id_type=MESH)

    def chord_down(i):
        return pltpu.make_async_remote_copy(
            src_ref=cslo.at[i], dst_ref=crhi.at[i], send_sem=cs.at[1, i], recv_sem=cq.at[1, i],
            device_id={"wrap": (wrap + WRAPS - 1) % WRAPS}, device_id_type=MESH)

    def fields(i, c):
        fringe_up(i).wait_recv()
        fringe_down(i).wait_recv()
        for s in range(S):
            marks = mk[s]
            outer = jnp.where(marks == 1, fb[i, s], jnp.where(marks == 2, fa[i, s], pk[i, s]))
            low = jnp.where(lane_h >= N // 2, pltpu.roll(outer, N // 2, 1), st[i, s, 0:H, :])
            high = jnp.where(lane_h >= N // 2, outer, st[i, s, H:W, :])
            fl[i, s, 8 : 8 + H, :] = low
            fl[i, s, 8 + H : 8 + W, :] = high
            cslo[i, 2 * s : 2 * s + 2, :] = low[0:2]
            cshi[i, 2 * s : 2 * s + 2, :] = high[H - 2 : H]
        chord_up(i).start()
        chord_down(i).start()
        halo_up(i).start()
        halo_down(i).start()
        return c

    lax.fori_loop(0, V, fields, 0)

    has_low = jnp.where(span > 0, 1.0, 0.0)
    has_high = jnp.where(span < SPANS - 1, 1.0, 0.0)

    def group_send(i, d):
        target = group * GROUP + (place + d) % GROUP
        return pltpu.make_async_remote_copy(
            src_ref=ms.at[i], dst_ref=m1.at[i, place], send_sem=r1s.at[i, d - 1], recv_sem=r1q.at[i, d - 1],
            device_id={"wrap": target}, device_id_type=MESH)

    def total_send(i, d):
        target = (group + d) % groups * GROUP + place
        return pltpu.make_async_remote_copy(
            src_ref=gs.at[i], dst_ref=m2.at[i, group], send_sem=r2s.at[i, d - 1], recv_sem=r2q.at[i, d - 1],
            device_id={"wrap": target}, device_id_type=MESH)

    def residuals(i, c):
        chord_up(i).wait_recv()
        chord_down(i).wait_recv()
        halo_up(i).wait_recv()
        halo_down(i).wait_recv()
        for s in range(S):
            fl[i, s, 6:8, :] = crlo[i, 2 * s : 2 * s + 2, :]
            fl[i, s, 8 + W : 10 + W, :] = crhi[i, 2 * s : 2 * s + 2, :]

        def station(t):
            if t < 0:
                return hlo[i, t + 2] * has_low
            if t >= S:
                return hhi[i, t - S] * has_high
            return fl[i, t, 8 : 8 + W, :]

        for s in range(S):
            own = fl[i, s, 8 : 8 + W, :]
            ahead = jnp.where(lane_w < N - 1, pltpu.roll(own, N - 1, 1), 0.0)
            behind = jnp.where(lane_w > 0, pltpu.roll(own, 1, 1), 0.0)
            wide = fl[i, s, 10 : 10 + W, :] + fl[i, s, 6 : 6 + W, :] + station(s + 2) + station(s - 2)
            plus = fl[i, s, 9 : 9 + W, :] + station(s + 1)
            minus = fl[i, s, 7 : 7 + W, :] + station(s - 1)
            rhs = (so[i, s] - 2.1 * own) + 0.25 * (ahead + behind) - 0.05 * wide - 0.3 * plus + 0.7 * minus
            fr[i, s] = rhs
            ms[i, 0, s : s + 1, :] = jnp.sum(gd[i, s, 0:W, :] * rhs, axis=0, keepdims=True)
            ms[i, 1, s : s + 1, :] = jnp.sum(gd[i, s, 1 : 1 + W, :] * rhs, axis=0, keepdims=True)
            ms[i, 0, S + s : S + s + 1, :] = jnp.sum(ga[i, s, 1 : 1 + W, :] * rhs, axis=0, keepdims=True)
            ms[i, 1, S + s : S + s + 1, :] = jnp.sum(ga[i, s, 0:W, :] * rhs, axis=0, keepdims=True)
        m1[i, place] = ms[i]
        for d in range(1, GROUP):
            group_send(i, d).start()
        return c

    lax.fori_loop(0, V, residuals, 0)

    def down(x, n):
        if n % 8 == 0:
            return jnp.concatenate([jnp.zeros((n, N), jnp.float32), x[: W - n]], axis=0)
        return jnp.where(row_w >= n, pltpu.roll(x, n, 0), 0.0)

    def up(x, n):
        if n % 8 == 0:
            return jnp.concatenate([x[n:], jnp.zeros((n, N), jnp.float32)], axis=0)
        return jnp.where(row_w < W - n, pltpu.roll(x, W - n, 0), 0.0)

    def sweeps(idx, c):
        i = idx // S
        s = idx % S
        rhs = fr[i, s]

        def coef(k):
            return cf[i, s, k : k + 1, :]

        ahead = coef(12) * rhs + coef(13) * down(rhs, 1)
        back = coef(14) * up(rhs, 1) + coef(15) * up(rhs, 2)
        for k in range(LEVELS):
            n = 1 << k
            pc, qc = coef(k), coef(LEVELS + k)
            if 2 * n < W:
                ahead = ahead + pc * down(ahead, n) + qc * down(ahead, 2 * n)
                back = back + pc * up(back, n) + qc * up(back, 2 * n)
            else:
                ahead = ahead + pc * down(ahead, n)
                back = back + pc * up(back, n)
        xb[i, s] = ahead + back
        return c

    lax.fori_loop(0, 2 * S, sweeps, 0)

    forward = row_8 < S
    steps = jnp.where(forward, place, GROUP - 1 - place)

    def advance(t, acc, x):
        return (t[0] * acc[0] + t[1] * acc[1] + x[0], t[2] * acc[0] + t[3] * acc[1] + x[1])

    def ordered(ref, i, a, b):
        return tuple(jnp.where(forward, ref[i, a, k], ref[i, b, k]) for k in range(2))

    zero_8 = jnp.zeros((8, N), jnp.float32)

    def totals(i, c):
        for d in range(1, GROUP):
            group_send(i, d).wait_recv()
        t = [tm[i, k] for k in range(4)]
        acc = (zero_8, zero_8)
        for j in range(GROUP):
            acc = advance(t, acc, ordered(m1, i, j, GROUP - 1 - j))
        gs[i, 0] = acc[0]
        gs[i, 1] = acc[1]
        m2[i, group, 0] = acc[0]
        m2[i, group, 1] = acc[1]
        for d in range(1, groups):
            total_send(i, d).start()
        return c

    lax.fori_loop(0, V, totals, 0)

    lax.fori_loop(2 * S, V * S, sweeps, 0)

    low_side = span < SPANS // 2
    inner = (span == 1) | (span == 2)
    outer_dev = (span == 0) | (span == SPANS - 1)
    mate = jnp.where(span % 2 == 0, span + 1, span - 1)

    def spot(j):
        return jnp.where(low_side, j, S - 1 - j)

    def y_copy(i):
        return pltpu.make_async_remote_copy(
            src_ref=ysend.at[i], dst_ref=yrecv.at[i], send_sem=ys.at[i], recv_sem=yq.at[i],
            device_id={"span": mate}, device_id_type=MESH)

    def a_copy(i):
        return pltpu.make_async_remote_copy(
            src_ref=asend.at[i], dst_ref=arecv.at[i], send_sem=as_.at[i], recv_sem=aq.at[i],
            device_id={"span": SPANS - 1 - span}, device_id_type=MESH)

    def x_copy(i):
        return pltpu.make_async_remote_copy(
            src_ref=xsend.at[i], dst_ref=xrecv.at[i], send_sem=xs.at[i], recv_sem=xq.at[i],
            device_id={"span": mate}, device_id_type=MESH)

    def carried(i, c):
        for d in range(1, groups):
            total_send(i, d).wait_recv()
        t = [tm[i, k] for k in range(4)]
        t4 = [tm[i, 4 + k] for k in range(4)]
        acc = (zero_8, zero_8)
        for turn in range(2):
            for d in range(groups, 0, -1):
                acc = advance(t4, acc, ordered(m2, i, (group + groups - d) % groups, (group + d) % groups))
        for j in range(GROUP - 1):
            nxt = advance(t, acc, ordered(m1, i, j, GROUP - 1 - j))
            acc = tuple(jnp.where(j < steps, b, a) for a, b in zip(acc, nxt))
        cc[0] = acc[0]
        cc[1] = acc[1]
        for s in range(S):
            minus_q = -cf[i, s, LEVELS : LEVELS + 1, :]
            xb[i, s] = (
                xb[i, s]
                + ub[i, s, 1 : 1 + W, :] * cc[0, s : s + 1, :]
                + ub[i, s, 0:W, :] * (minus_q * cc[1, s : s + 1, :])
                + ud[i, s, 0:W, :] * cc[0, S + s : S + s + 1, :]
                + ud[i, s, 1 : 1 + W, :] * (minus_q * cc[1, S + s : S + s + 1, :])
            )

        @pl.when(outer_dev)
        def _():
            y = []
            for j in range(S):
                now = xb[i, spot(j)]
                if j >= 1:
                    now = now - l1t[i, j] * y[j - 1]
                if j >= 2:
                    now = now - l2t[i, j] * y[j - 2]
                y.append(now)
                xb[i, spot(j)] = now * rdt[i, j]
            ysend[i, 0] = y[S - 2]
            ysend[i, 1] = y[S - 1]
            y_copy(i).start()

        return c

    lax.fori_loop(0, V, carried, 0)

    def inner_forward(i, c):
        y_copy(i).wait_recv()
        y = [yrecv[i, 0], yrecv[i, 1]]
        for j in range(S):
            now = xb[i, spot(j)] - l1t[i, S + j] * y[-1] - l2t[i, S + j] * y[-2]
            y.append(now)
            scaled = now * rdt[i, S + j]
            xb[i, spot(j)] = scaled
            if j >= S - 2:
                asend[i, j - (S - 2)] = scaled
        a_copy(i).start()
        return c

    @pl.when(inner)
    def _():
        lax.fori_loop(0, V, inner_forward, 0)

    def out_copy(i):
        return pltpu.make_async_copy(ob.at[i], out.at[0, var_of(i)], out_s.at[i])

    def finish(i, j, x):
        at = spot(j)
        ob[i, at] = fl[i, at, 8 : 8 + W, :] + x

    def inner_back(i, c):
        a_copy(i).wait_recv()
        a6, a7 = xb[i, spot(2)], xb[i, spot(3)]
        b6, b7 = arecv[i, 0], arecv[i, 1]
        l29 = l2t[i, 9]
        lead = a7 - l29 * b6
        other = b7 - l29 * a6
        x7 = alt[i] * lead - bet[i] * other
        x8 = alt[i] * other - bet[i] * lead
        x6 = a6 - l1t[i, 7] * x7 - l2t[i, 8] * x8
        x5 = xb[i, spot(1)] - l1t[i, 6] * x6 - l2t[i, 7] * x7
        x4 = xb[i, spot(0)] - l1t[i, 5] * x5 - l2t[i, 6] * x6
        xsend[i, 0] = x4
        xsend[i, 1] = x5
        x_copy(i).start()
        for j, x in enumerate((x4, x5, x6, x7)):
            finish(i, j, x)
        out_copy(i).start()
        return c

    def outer_back(i, c):
        x_copy(i).wait_recv()
        x = [xrecv[i, 1], xrecv[i, 0]]
        for j in range(S - 1, -1, -1):
            now = xb[i, spot(j)] - l1t[i, j + 1] * x[-1] - l2t[i, j + 2] * x[-2]
            x.append(now)
            finish(i, j, now)
        out_copy(i).start()
        return c

    def back(first, last):
        @pl.when(inner)
        def _():
            lax.fori_loop(first, last, inner_back, 0)

        @pl.when(outer_dev)
        def _():
            lax.fori_loop(first, last, outer_back, 0)

    back(0, 3)

    part = SECTIONS // SPANS
    padded = 256
    total = jnp.zeros((8, SPANS * padded), jnp.float32)
    spots = lax.broadcasted_iota(jnp.int32, (SPANS * padded, W), 0)
    for s in range(S):
        wall = jnp.zeros((W, N), jnp.float32)
        for k in range(3):
            value = ob[k, s]
            step = pltpu.roll(value, N - 1, 1) - value
            if k:
                step = pltpu.roll(step, k, 1)
            wall = jnp.where(lane_w == k, step, wall)
        names = sec[s : s + 1, :]
        for k in range(1, SPANS):
            names = names + jnp.where(sec[s : s + 1, :] >= k * part, padded - part, 0)
        picks = jnp.where(spots == names, 1.0, 0.0)
        total = total + lax.dot_general(
            jnp.transpose(wall)[0:8, :], picks, (((1,), (1,)), ((), ())),
            precision=lax.Precision.HIGHEST, preferred_element_type=jnp.float32)
    for k in range(SPANS):
        la[k] = total[:, k * padded : (k + 1) * padded]

    def load_span(d):
        return pltpu.make_async_remote_copy(
            src_ref=la.at[(span + d) % SPANS], dst_ref=lra.at[d - 1], send_sem=las.at[d - 1], recv_sem=laq.at[d - 1],
            device_id={"span": (span + d) % SPANS}, device_id_type=MESH)

    for d in range(1, SPANS):
        load_span(d).start()

    back(3, V)

    for d in range(1, SPANS):
        load_span(d).wait_recv()
    mine = la[span]
    for d in range(1, SPANS):
        mine = mine + lra[d - 1]
    each = part // WRAPS
    for k in range(WRAPS):
        ld[k] = (mine if k == 0 else pltpu.roll(mine, padded - each * k, 1))[:, 0:N]

    def load_wrap(d):
        target = (wrap + d) % WRAPS
        return pltpu.make_async_remote_copy(
            src_ref=ld.at[target], dst_ref=lrb.at[d - 1], send_sem=lbs.at[d - 1], recv_sem=lbq.at[d - 1],
            device_id={"wrap": target}, device_id_type=MESH)

    def load_start(d, c):
        load_wrap(d).start()
        return c

    lax.fori_loop(1, WRAPS, load_start, 0)

    def drain(i, c):
        fringe_up(i).wait_send()
        fringe_down(i).wait_send()
        halo_up(i).wait_send()
        halo_down(i).wait_send()
        chord_up(i).wait_send()
        chord_down(i).wait_send()
        for d in range(1, GROUP):
            group_send(i, d).wait_send()
        for d in range(1, groups):
            total_send(i, d).wait_send()
        out_copy(i).wait()
        return c

    lax.fori_loop(0, V, drain, 0)

    @pl.when(inner)
    def _():
        def body(i, c):
            a_copy(i).wait_send()
            x_copy(i).wait_send()
            return c

        lax.fori_loop(0, V, body, 0)

    @pl.when(outer_dev)
    def _():
        def body(i, c):
            y_copy(i).wait_send()
            return c

        lax.fori_loop(0, V, body, 0)

    for d in range(1, SPANS):
        load_span(d).wait_send()

    def load_end(d, acc):
        load_wrap(d).wait()
        return acc + lrb[d - 1]

    final = lax.fori_loop(1, WRAPS, load_end, ld[wrap])
    loads[0] = final[0:3, 0:each]


def local(state, state_old, wrap_rate, span_rate, blank, section):
    def vm(*shape):
        return pltpu.VMEM(shape, jnp.float32)

    def im(*shape):
        return pltpu.VMEM(shape, jnp.int32)

    dma = pltpu.SemaphoreType.DMA
    scratch = [
        vm(V, S, W, N), vm(V, S, W, N), vm(V, S, N), vm(V, W, N), im(S, W, N // 2), im(S, H, N), im(S, W),
        vm(V, S, H, N), vm(V, S, H, N), vm(V, S, H, N), vm(V, S, W + 16, N),
        vm(V, 2, W, N), vm(V, 2, W, N), vm(V, 8, N), vm(V, 8, N), vm(V, 8, N), vm(V, 8, N), vm(V, S, W, N),
        vm(V, S, W + 8, N), vm(V, S, W + 8, N), vm(V, S, W + 8, N), vm(V, S, W + 8, N), vm(V, S, 16, N),
        vm(8, N), vm(V, 8, 8, N), vm(V, 2, 8, N), vm(V, GROUP, 2, 8, N), vm(V, 2, 8, N), vm(V, WRAPS // GROUP, 2, 8, N),
        vm(2, 8, N), vm(V, S, W, N), vm(V, 9, W, N), vm(V, 10, W, N), vm(V, 8, W, N), vm(V, W, N), vm(V, W, N),
        vm(V, 2, W, N), vm(V, 2, W, N), vm(V, 2, W, N), vm(V, 2, W, N), vm(V, 2, W, N), vm(V, 2, W, N),
        vm(V, S, W, N), vm(SPANS, 8, 256), vm(SPANS - 1, 8, 256), vm(WRAPS, 8, N), vm(WRAPS - 1, 8, N),
        dma((13,)), dma((V,)), dma((V,)), dma((2, V)), dma((2, V)), dma((2, V)), dma((2, V)), dma((2, V)), dma((2, V)),
        dma((V, GROUP - 1)), dma((V, GROUP - 1)), dma((V, 3)), dma((V, 3)),
        dma((V,)), dma((V,)), dma((V,)), dma((V,)), dma((V,)), dma((V,)),
        dma((SPANS - 1,)), dma((SPANS - 1,)), dma((WRAPS - 1,)), dma((WRAPS - 1,)),
    ]
    each = SECTIONS // (SPANS * WRAPS)
    return pl.pallas_call(
        kernel,
        out_shape=(
            jax.ShapeDtypeStruct(state.shape, jnp.float32),
            jax.ShapeDtypeStruct((1, 3, each), jnp.float32),
        ),
        in_specs=[pl.BlockSpec(memory_space=pl.ANY)] * 6,
        out_specs=(pl.BlockSpec(memory_space=pl.ANY), pl.BlockSpec(memory_space=pltpu.VMEM)),
        scratch_shapes=scratch,
        compiler_params=pltpu.CompilerParams(
            collective_id=0, has_side_effects=True, vmem_limit_bytes=48 * 1024 * 1024),
    )(state, state_old, wrap_rate, span_rate, blank, section)


def solution(mesh):
    return jax.shard_map(
        local,
        mesh=mesh,
        in_specs=(
            P("blade", None, "span", "wrap", None),
            P("blade", None, "span", "wrap", None),
            P("blade", None, "span", None),
            P("blade", None, "wrap", None),
            P("blade", "span", "wrap", None),
            P("blade", "span", "wrap"),
        ),
        out_specs=(P("blade", None, "span", "wrap", None), P("blade", None, ("span", "wrap"))),
        check_vma=False,
    )
```

```python
import jax
import jax.numpy as jnp
from jax import lax
from jax.experimental import pallas as pl
from jax.experimental.pallas import tpu as pltpu
from jax.sharding import PartitionSpec as P

MESH = pl.DeviceIdType.MESH
SECTIONS = 640
V, S, W, N = 5, 4, 64, 128
Q = V + 1
H = W // 2
GROUP = 4
SPANS, WRAPS, BLADES = 4, 16, 4
LEVELS = 6


def line_roots(r):
    ri = 1.0 / r
    y = 6.0 + ri + jnp.sqrt(ri * (12.0 + ri))
    q = 2.0 / ((y - 2.0) + jnp.sqrt(y * (y - 4.0)))
    p = 6.0 * q / (1.0 + q)
    return p, q


def square(m):
    a, b, c, d = m
    bc = b * c
    tr = a + d
    return a * a + bc, b * tr, c * tr, d * d + bc


RESIDUAL, TOTAL, CARRY, INNER_AHEAD, INNER_BACK, OUTER_BACK = 3, 5, 8, 10, 12, 14
WALL_TICKS = (1, 3, 6, 8, 10, 12)
LOAD_PART, LOAD_SUM = 13, 15


def kernel(
    state, old, wrate, srate, blank, section,
    out, loads,
    st, so, wr, sr, bl, mk, sec, pk, lk, op, fb, fa, fl, hlo, hhi, llo, lhi, olo, ohi, cslo, cshi, crlo, crhi, fr,
    ga, gd, ub, ud, cf, r8, tm, ms, m1, gs, m2, cc, xb, l1t, l2t, rdt, alt, bet,
    ysend, yrecv, asend, arecv, xsend, xrecv, ob, la, lra, ld, lrb,
    in_s, st_s, out_s, fs, fq, hs, hq, ls, lq, os_, oq, cs, cq, r1s, r1q, r2s, r2q, ys, yq, as_, aq, xs, xq,
    las, laq, lbs, lbq,
):
    span = lax.axis_index("span")
    wrap = lax.axis_index("wrap")
    blade = lax.axis_index("blade")
    place = wrap % GROUP
    group = wrap // GROUP
    groups = WRAPS // GROUP

    barrier = pltpu.get_barrier_semaphore()
    for d in range(1, WRAPS):
        pl.semaphore_signal(barrier, inc=1, device_id={"wrap": (wrap + d) % WRAPS}, device_id_type=MESH)
    for d in range(1, SPANS):
        pl.semaphore_signal(barrier, inc=1, device_id={"span": (span + d) % SPANS}, device_id_type=MESH)
    for d in (1, BLADES - 1):
        pl.semaphore_signal(barrier, inc=1, device_id={"blade": (blade + d) % BLADES}, device_id_type=MESH)

    copy_wr = pltpu.make_async_copy(wrate.at[0], wr.at[1:Q], in_s.at[0])
    copy_st = [pltpu.make_async_copy(state.at[0, v], st.at[v + 1], st_s.at[v]) for v in range(V)]
    copy_bl = pltpu.make_async_copy(blank.at[0], bl, in_s.at[1])
    copy_sr = pltpu.make_async_copy(srate.at[0], sr.at[1:Q], in_s.at[2])
    copy_so = pltpu.make_async_copy(old.at[0], so.at[1:Q], in_s.at[3])
    copy_sec = pltpu.make_async_copy(section.at[0], sec, in_s.at[4])
    for copy in [copy_wr] + copy_st + [copy_bl, copy_sr, copy_so, copy_sec]:
        copy.start()

    lane_h = lax.broadcasted_iota(jnp.int32, (H, N), 1)
    lane_w = lax.broadcasted_iota(jnp.int32, (W, N), 1)
    row_w = lax.broadcasted_iota(jnp.int32, (W, N), 0)
    row_8 = lax.broadcasted_iota(jnp.int32, (8, N), 0)

    def wall_lanes(a, b, c, rest):
        lane = lax.broadcasted_iota(jnp.int32, a.shape, 1)
        return jnp.where(
            lane < 4, a, jnp.where(lane < 8, pltpu.roll(b, 4, 1), jnp.where(lane < 12, pltpu.roll(c, 8, 1), rest)))

    copy_wr.wait()
    wr[0] = wall_lanes(wr[2], wr[3], wr[4], 1.0)

    def chord_tables(idx, c):
        i = idx // S
        s = idx % S
        r = jnp.broadcast_to(wr[i, pl.ds(s, 1), :], (8, N))
        p, q = line_roots(r)
        g0 = (1.0 + q) * (2.0 * q) / (r * (1.0 - q) * (1.0 + q - p) * (1.0 + q + p))
        ratio = p / (1.0 + q)
        g1 = g0 * ratio
        pk_, qk_ = [p], [q]
        for k in range(LEVELS - 1):
            pk_.append(pk_[-1] * pk_[-1] - 2.0 * qk_[-1])
            qk_.append(qk_[-1] * qk_[-1])
        rows = pk_ + qk_ + [g0, -g1 * q, g1, -q * g0]

        def pick(values):
            tile = values[0]
            for n in range(1, 8):
                tile = jnp.where(row_8 == n, values[n], tile)
            return tile

        cf[i, s, 0:8, :] = pick(rows[0:8])
        cf[i, s, 8:16, :] = pick(rows[8:16])
        g = [g0, g1]
        for n in range(2, 17):
            g.append(p * g[-1] - q * g[-2])
        zero = jnp.zeros_like(p)
        u = [zero, zero + 1.0]
        for n in range(2, 17):
            u.append(p * u[-1] - q * u[-2])
        p3, q3 = pk_[3], qk_[3]

        def ascend(table, first, second):
            table[i, s, 0:8, :] = first
            table[i, s, 8:16, :] = second
            before, now = first, second
            for t in range(2, 9):
                before, now = now, p3 * now - q3 * before
                table[i, s, 8 * t : 8 * t + 8, :] = now

        def descend(table, last, first, second):
            table[i, s, 64:72, :] = last
            table[i, s, 56:64, :] = first
            table[i, s, 48:56, :] = second
            before, now = first, second
            for t in range(5, -1, -1):
                before, now = now, p3 * now - q3 * before
                table[i, s, 8 * t : 8 * t + 8, :] = now

        ascend(ga, pick(g[0:8]), pick(g[8:16]))
        descend(gd, jnp.where(row_8 == 0, g0, 0.0), pick(g[8:0:-1]), pick(g[16:8:-1]))
        ascend(ub, pick(u[0:8]), pick(u[8:16]))
        descend(ud, zero, pick(u[8:0:-1]), pick(u[16:8:-1]))
        return c

    lax.fori_loop(0, Q * S, chord_tables, 0)

    for copy in copy_st:
        copy.wait()

    def pack(i, c):
        for s in range(S):
            low = st[i, s, 0:H, :]
            high = st[i, s, H:W, :]
            pk[i, s] = jnp.where(lane_h < N // 2, pltpu.roll(low, N // 2, 1), high)
            lk[i, s] = jnp.where(lane_h < N // 2, low, pltpu.roll(high, N // 2, 1))
        return c

    lax.fori_loop(1, Q, pack, 0)

    for s in range(S):
        wall = wall_lanes(st[2, s], st[3, s], st[4, s], 0.0)
        fl[0, s, 8 : 8 + W, :] = wall
        cslo[0, 2 * s : 2 * s + 2, :] = wall[0:2]
        cshi[0, 2 * s : 2 * s + 2, :] = wall[W - 2 : W]

    def fringe_up(i):
        return pltpu.make_async_remote_copy(
            src_ref=pk.at[i], dst_ref=fb.at[i], send_sem=fs.at[0, i], recv_sem=fq.at[0, i],
            device_id={"blade": (blade + 1) % BLADES}, device_id_type=MESH)

    def fringe_down(i):
        return pltpu.make_async_remote_copy(
            src_ref=pk.at[i], dst_ref=fa.at[i], send_sem=fs.at[1, i], recv_sem=fq.at[1, i],
            device_id={"blade": (blade + BLADES - 1) % BLADES}, device_id_type=MESH)

    above = (span + 1) % SPANS
    below = (span + SPANS - 1) % SPANS

    def wall_up():
        return pltpu.make_async_remote_copy(
            src_ref=fl.at[0, 2:4, 8 : 8 + W, :], dst_ref=hlo.at[0], send_sem=hs.at[0], recv_sem=hq.at[0],
            device_id={"span": above}, device_id_type=MESH)

    def wall_down():
        return pltpu.make_async_remote_copy(
            src_ref=fl.at[0, 0:2, 8 : 8 + W, :], dst_ref=hhi.at[0], send_sem=hs.at[1], recv_sem=hq.at[1],
            device_id={"span": below}, device_id_type=MESH)

    def low_up(i):
        return pltpu.make_async_remote_copy(
            src_ref=lk.at[i, 2:4], dst_ref=llo.at[i], send_sem=ls.at[0, i], recv_sem=lq.at[0, i],
            device_id={"span": above}, device_id_type=MESH)

    def low_down(i):
        return pltpu.make_async_remote_copy(
            src_ref=lk.at[i, 0:2], dst_ref=lhi.at[i], send_sem=ls.at[1, i], recv_sem=lq.at[1, i],
            device_id={"span": below}, device_id_type=MESH)

    def outer_up(i):
        return pltpu.make_async_remote_copy(
            src_ref=op.at[i, 2:4], dst_ref=olo.at[i], send_sem=os_.at[0, i], recv_sem=oq.at[0, i],
            device_id={"span": above}, device_id_type=MESH)

    def outer_down(i):
        return pltpu.make_async_remote_copy(
            src_ref=op.at[i, 0:2], dst_ref=ohi.at[i], send_sem=os_.at[1, i], recv_sem=oq.at[1, i],
            device_id={"span": below}, device_id_type=MESH)

    def chord_up(i):
        return pltpu.make_async_remote_copy(
            src_ref=cshi.at[i], dst_ref=crlo.at[i], send_sem=cs.at[0, i], recv_sem=cq.at[0, i],
            device_id={"wrap": (wrap + 1) % WRAPS}, device_id_type=MESH)

    def chord_down(i):
        return pltpu.make_async_remote_copy(
            src_ref=cslo.at[i], dst_ref=crhi.at[i], send_sem=cs.at[1, i], recv_sem=cq.at[1, i],
            device_id={"wrap": (wrap + WRAPS - 1) % WRAPS}, device_id_type=MESH)

    def group_send(i, d):
        target = group * GROUP + (place + d) % GROUP
        return pltpu.make_async_remote_copy(
            src_ref=ms.at[i], dst_ref=m1.at[i, place], send_sem=r1s.at[i, d - 1], recv_sem=r1q.at[i, d - 1],
            device_id={"wrap": target}, device_id_type=MESH)

    def total_send(i, d):
        peer = GROUP - 1 - place if d % 2 else place
        target = (group + d) % groups * GROUP + peer
        return pltpu.make_async_remote_copy(
            src_ref=gs.at[i], dst_ref=m2.at[i, group], send_sem=r2s.at[i, d - 1], recv_sem=r2q.at[i, d - 1],
            device_id={"wrap": target}, device_id_type=MESH)

    pl.semaphore_wait(barrier, 2 + SPANS - 1 + WRAPS - 1)

    def first_sends(i, c):
        fringe_up(i).start()
        fringe_down(i).start()
        low_up(i).start()
        low_down(i).start()
        return c

    wall_up().start()
    wall_down().start()
    chord_up(0).start()
    chord_down(0).start()
    lax.fori_loop(1, Q, first_sends, 0)

    for copy in (copy_bl, copy_sr, copy_so, copy_sec):
        copy.wait()

    for s in range(S):
        mk[s] = jnp.concatenate([bl[s, 0:H, :], bl[s, H:W, :]], axis=-1)
        so[0, s] = wall_lanes(so[2, s], so[3, s], so[4, s], 0.0)
    sr[0] = wall_lanes(sr[2], sr[3], sr[4], 1.0)

    def transfers(i, c):
        rate = wr[i]
        r8[0:S, :] = rate
        r8[S : 2 * S, :] = rate
        p, q = line_roots(r8[...])
        m = (p, -q, jnp.ones_like(p), jnp.zeros_like(p))
        for k in range(LEVELS):
            m = square(m)
        for k in range(4):
            tm[i, k] = m[k]
        m = square(square(m))
        for k in range(4):
            tm[i, 4 + k] = m[k]
        return c

    lax.fori_loop(0, Q, transfers, 0)

    def span_tables(idx, c):
        i = idx // 8
        rows = pl.ds(pl.multiple_of((idx % 8) * 8, 8), 8)
        r = sr[i, rows, :]
        centre = 1.0 + 5.0 * r
        first = -3.0 * r
        second = 0.5 * r
        zero = jnp.zeros_like(r)
        one_l, two_l, rd = [zero], [zero], [1.0 / centre]
        for j in range(1, 10):
            two = second * rd[j - 2] if j >= 2 else zero
            two_l.append(two)
            if j == 9:
                break
            top = first - second * one_l[j - 1]
            one = top * rd[j - 1]
            one_l.append(one)
            if j < 8:
                rd.append(1.0 / (centre - one * top - two * second))
        for j in range(9):
            l1t[i, j, rows, :] = one_l[j]
        for j in range(10):
            l2t[i, j, rows, :] = two_l[j]
        for j in range(8):
            rdt[i, j, rows, :] = rd[j]
        alpha = 1.0 - two_l[9] * two_l[8]
        beta = one_l[8] - two_l[9] * one_l[7]
        det = 1.0 / ((alpha - beta) * (alpha + beta))
        alt[i, rows, :] = alpha * det
        bet[i, rows, :] = beta * det
        return c

    lax.fori_loop(0, Q * 8, span_tables, 0)

    def fields(i):
        fringe_up(i).wait_recv()
        fringe_down(i).wait_recv()
        for s in range(S):
            marks = mk[s]
            op[i, s] = jnp.where(marks == 1, fb[i, s], jnp.where(marks == 2, fa[i, s], pk[i, s]))
        outer_up(i).start()
        outer_down(i).start()
        for s in range(S):
            outer = op[i, s]
            low = jnp.where(lane_h >= N // 2, pltpu.roll(outer, N // 2, 1), st[i, s, 0:H, :])
            high = jnp.where(lane_h >= N // 2, outer, st[i, s, H:W, :])
            fl[i, s, 8 : 8 + H, :] = low
            fl[i, s, 8 + H : 8 + W, :] = high
            cslo[i, 2 * s : 2 * s + 2, :] = low[0:2]
            cshi[i, 2 * s : 2 * s + 2, :] = high[H - 2 : H]
        chord_up(i).start()
        chord_down(i).start()

    has_low = jnp.where(span > 0, 1.0, 0.0)
    has_high = jnp.where(span < SPANS - 1, 1.0, 0.0)

    def residuals(i):
        chord_up(i).wait_recv()
        chord_down(i).wait_recv()

        @pl.when(i == 0)
        def _():
            wall_up().wait_recv()
            wall_down().wait_recv()

        @pl.when(i > 0)
        def _():
            low_up(i).wait_recv()
            low_down(i).wait_recv()
            outer_up(i).wait_recv()
            outer_down(i).wait_recv()
            for low, outer, whole in ((llo, olo, hlo), (lhi, ohi, hhi)):
                for k in range(2):
                    whole[i, k, 0:H, :] = jnp.where(lane_h < N // 2, low[i, k], pltpu.roll(outer[i, k], N // 2, 1))
                    whole[i, k, H:W, :] = jnp.where(lane_h < N // 2, pltpu.roll(low[i, k], N // 2, 1), outer[i, k])

        for s in range(S):
            fl[i, s, 6:8, :] = crlo[i, 2 * s : 2 * s + 2, :]
            fl[i, s, 8 + W : 10 + W, :] = crhi[i, 2 * s : 2 * s + 2, :]

        def station(t):
            if t < 0:
                return hlo[i, t + 2] * has_low
            if t >= S:
                return hhi[i, t - S] * has_high
            return fl[i, t, 8 : 8 + W, :]

        inside = (lane_w & jnp.where(i == 0, 3, N - 1)) > 0
        for s in range(S):
            own = fl[i, s, 8 : 8 + W, :]
            ahead = jnp.where(lane_w < N - 1, pltpu.roll(own, N - 1, 1), 0.0)
            behind = jnp.where(inside, pltpu.roll(own, 1, 1), 0.0)
            wide = fl[i, s, 10 : 10 + W, :] + fl[i, s, 6 : 6 + W, :] + station(s + 2) + station(s - 2)
            plus = fl[i, s, 9 : 9 + W, :] + station(s + 1)
            minus = fl[i, s, 7 : 7 + W, :] + station(s - 1)
            rhs = (so[i, s] - 2.1 * own) + 0.25 * (ahead + behind) - 0.05 * wide - 0.3 * plus + 0.7 * minus
            fr[i, s] = rhs
            ms[i, 0, s : s + 1, :] = jnp.sum(gd[i, s, 0:W, :] * rhs, axis=0, keepdims=True)
            ms[i, 1, s : s + 1, :] = jnp.sum(gd[i, s, 1 : 1 + W, :] * rhs, axis=0, keepdims=True)
            ms[i, 0, S + s : S + s + 1, :] = jnp.sum(ga[i, s, 1 : 1 + W, :] * rhs, axis=0, keepdims=True)
            ms[i, 1, S + s : S + s + 1, :] = jnp.sum(ga[i, s, 0:W, :] * rhs, axis=0, keepdims=True)
        m1[i, place] = ms[i]
        for d in range(1, GROUP):
            group_send(i, d).start()

    def down(x, n):
        if n % 8 == 0:
            return jnp.concatenate([jnp.zeros((n, N), jnp.float32), x[: W - n]], axis=0)
        return jnp.where(row_w >= n, pltpu.roll(x, n, 0), 0.0)

    def up(x, n):
        if n % 8 == 0:
            return jnp.concatenate([x[n:], jnp.zeros((n, N), jnp.float32)], axis=0)
        return jnp.where(row_w < W - n, pltpu.roll(x, W - n, 0), 0.0)

    def sweeps(i, s):
        rhs = fr[i, s]

        def coef(k):
            return cf[i, s, k : k + 1, :]

        ahead = coef(12) * rhs + coef(13) * down(rhs, 1)
        back = coef(14) * up(rhs, 1) + coef(15) * up(rhs, 2)
        for k in range(LEVELS):
            n = 1 << k
            pc, qc = coef(k), coef(LEVELS + k)
            if 2 * n < W:
                ahead = ahead + pc * down(ahead, n) + qc * down(ahead, 2 * n)
                back = back + pc * up(back, n) + qc * up(back, 2 * n)
            else:
                ahead = ahead + pc * down(ahead, n)
                back = back + pc * up(back, n)
        xb[i, s] = ahead + back

    forward = row_8 < S
    steps = jnp.where(forward, place, GROUP - 1 - place)
    zero_8 = jnp.zeros((8, N), jnp.float32)

    def advance(t, acc, x):
        return (t[0] * acc[0] + t[1] * acc[1] + x[0], t[2] * acc[0] + t[3] * acc[1] + x[1])

    def ordered(ref, i, a, b):
        return tuple(jnp.where(forward, ref[i, a, k], ref[i, b, k]) for k in range(2))

    def totals(i):
        for d in range(1, GROUP):
            group_send(i, d).wait_recv()
        t = [tm[i, k] for k in range(4)]
        acc = (zero_8, zero_8)
        for j in range(GROUP):
            acc = advance(t, acc, ordered(m1, i, j, GROUP - 1 - j))
        gs[i, 0] = acc[0]
        gs[i, 1] = acc[1]
        for d in range(1, groups):
            total_send(i, d).start()
        m2[i, group, 0] = acc[0]
        m2[i, group, 1] = acc[1]

    low_side = span < SPANS // 2
    inner = (span == 1) | (span == 2)
    outer_dev = (span == 0) | (span == SPANS - 1)
    mate = jnp.where(span % 2 == 0, span + 1, span - 1)

    def spot(j):
        return jnp.where(low_side, j, S - 1 - j)

    def y_copy(i):
        return pltpu.make_async_remote_copy(
            src_ref=ysend.at[i], dst_ref=yrecv.at[i], send_sem=ys.at[i], recv_sem=yq.at[i],
            device_id={"span": mate}, device_id_type=MESH)

    def a_copy(i):
        return pltpu.make_async_remote_copy(
            src_ref=asend.at[i], dst_ref=arecv.at[i], send_sem=as_.at[i], recv_sem=aq.at[i],
            device_id={"span": SPANS - 1 - span}, device_id_type=MESH)

    def x_copy(i):
        return pltpu.make_async_remote_copy(
            src_ref=xsend.at[i], dst_ref=xrecv.at[i], send_sem=xs.at[i], recv_sem=xq.at[i],
            device_id={"span": mate}, device_id_type=MESH)

    def carried(i):
        for d in range(1, groups):
            total_send(i, d).wait_recv()
        t = [tm[i, k] for k in range(4)]
        t4 = [tm[i, 4 + k] for k in range(4)]
        acc = (zero_8, zero_8)
        for turn in range(2):
            for d in range(groups, 0, -1):
                acc = advance(t4, acc, ordered(m2, i, (group + groups - d) % groups, (group + d) % groups))
        for j in range(GROUP - 1):
            nxt = advance(t, acc, ordered(m1, i, j, GROUP - 1 - j))
            acc = tuple(jnp.where(j < steps, b, a) for a, b in zip(acc, nxt))
        cc[0] = acc[0]
        cc[1] = acc[1]
        for s in range(S):
            minus_q = -cf[i, s, LEVELS : LEVELS + 1, :]
            xb[i, s] = (
                xb[i, s]
                + ub[i, s, 1 : 1 + W, :] * cc[0, s : s + 1, :]
                + ub[i, s, 0:W, :] * (minus_q * cc[1, s : s + 1, :])
                + ud[i, s, 0:W, :] * cc[0, S + s : S + s + 1, :]
                + ud[i, s, 1 : 1 + W, :] * (minus_q * cc[1, S + s : S + s + 1, :])
            )

        @pl.when(outer_dev)
        def _():
            y = []
            for j in range(S):
                now = xb[i, spot(j)]
                if j >= 1:
                    now = now - l1t[i, j] * y[j - 1]
                if j >= 2:
                    now = now - l2t[i, j] * y[j - 2]
                y.append(now)
                xb[i, spot(j)] = now * rdt[i, j]
            ysend[i, 0] = y[S - 2]
            ysend[i, 1] = y[S - 1]
            y_copy(i).start()

    def inner_forward(i):
        y_copy(i).wait_recv()
        y = [yrecv[i, 0], yrecv[i, 1]]
        for j in range(S):
            now = xb[i, spot(j)] - l1t[i, S + j] * y[-1] - l2t[i, S + j] * y[-2]
            y.append(now)
            scaled = now * rdt[i, S + j]
            xb[i, spot(j)] = scaled
            if j >= S - 2:
                asend[i, j - (S - 2)] = scaled
        a_copy(i).start()

    def out_copy(i):
        return pltpu.make_async_copy(ob.at[i], out.at[0, i - 1], out_s.at[i])

    def finish(i, j, x):
        at = spot(j)
        ob[i, at] = fl[i, at, 8 : 8 + W, :] + x

    def leave(i):
        @pl.when(i > 0)
        def _():
            out_copy(i).start()

    def inner_back(i):
        a_copy(i).wait_recv()
        a6, a7 = xb[i, spot(2)], xb[i, spot(3)]
        b6, b7 = arecv[i, 0], arecv[i, 1]
        l29 = l2t[i, 9]
        lead = a7 - l29 * b6
        other = b7 - l29 * a6
        x7 = alt[i] * lead - bet[i] * other
        x8 = alt[i] * other - bet[i] * lead
        x6 = a6 - l1t[i, 7] * x7 - l2t[i, 8] * x8
        x5 = xb[i, spot(1)] - l1t[i, 6] * x6 - l2t[i, 7] * x7
        x4 = xb[i, spot(0)] - l1t[i, 5] * x5 - l2t[i, 6] * x6
        xsend[i, 0] = x4
        xsend[i, 1] = x5
        x_copy(i).start()
        for j, x in enumerate((x4, x5, x6, x7)):
            finish(i, j, x)
        leave(i)

    def outer_back(i):
        x_copy(i).wait_recv()
        x = [xrecv[i, 1], xrecv[i, 0]]
        for j in range(S - 1, -1, -1):
            now = xb[i, spot(j)] - l1t[i, j + 1] * x[-1] - l2t[i, j + 2] * x[-2]
            x.append(now)
            finish(i, j, now)
        leave(i)

    part = SECTIONS // SPANS
    padded = 256
    each = part // WRAPS

    def load_span(d):
        return pltpu.make_async_remote_copy(
            src_ref=la.at[(span + d) % SPANS], dst_ref=lra.at[d - 1], send_sem=las.at[d - 1], recv_sem=laq.at[d - 1],
            device_id={"span": (span + d) % SPANS}, device_id_type=MESH)

    def load_wrap(d):
        target = (wrap + d) % WRAPS
        return pltpu.make_async_remote_copy(
            src_ref=ld.at[target], dst_ref=lrb.at[d - 1], send_sem=lbs.at[d - 1], recv_sem=lbq.at[d - 1],
            device_id={"wrap": target}, device_id_type=MESH)

    def load_parts():
        walls, names = [], []
        for s in range(S):
            value = ob[0, s]
            step = pltpu.roll(value, N - 1, 1) - value
            wall = jnp.where(
                lane_w == 0, step, jnp.where(
                    lane_w == 1, pltpu.roll(step, N - 3, 1), jnp.where(
                        lane_w == 2, pltpu.roll(step, N - 6, 1), 0.0)))
            walls.append(jnp.transpose(wall)[0:8, :])
            name = sec[s : s + 1, :]
            for k in range(1, SPANS):
                name = name + jnp.where(sec[s : s + 1, :] >= k * part, padded - part, 0)
            names.append(name)
        nodes = jnp.concatenate(walls, axis=1)
        spots = lax.broadcasted_iota(jnp.int32, (SPANS * padded, S * W), 0)
        picks = jnp.where(spots == jnp.concatenate(names, axis=1), 1.0, 0.0).astype(jnp.bfloat16)
        parts = []
        for k in range(3):
            piece = nodes.astype(jnp.bfloat16)
            nodes = nodes - piece.astype(jnp.float32)
            parts.append(piece.astype(jnp.float32))
        stacked = jnp.concatenate(parts + [jnp.zeros_like(nodes)], axis=0).astype(jnp.bfloat16)
        sums = lax.dot_general(
            stacked, picks, (((1,), (1,)), ((), ())), preferred_element_type=jnp.float32)
        total = sums[0:8] + sums[8:16] + sums[16:24]
        for k in range(SPANS):
            la[k] = total[:, k * padded : (k + 1) * padded]
        for d in range(1, SPANS):
            load_span(d).start()

    def load_sums():
        for d in range(1, SPANS):
            load_span(d).wait_recv()
        mine = la[span]
        for d in range(1, SPANS):
            mine = mine + lra[d - 1]
        for k in range(WRAPS):
            ld[k] = (mine if k == 0 else pltpu.roll(mine, padded - each * k, 1))[:, 0:N]

        def load_start(d, c):
            load_wrap(d).start()
            return c

        lax.fori_loop(1, WRAPS, load_start, 0)

    def tick(t, c):
        def stage(offset, wall, body, role=True):
            i = jnp.where(t == wall, 0, t - offset)

            @pl.when(((t == wall) | ((i >= 1) & (i < Q))) & role)
            def _():
                body(i)

        def chord_stage(i):
            residuals(i)

            def one(s, c):
                sweeps(i, s)
                return c

            lax.fori_loop(0, S, one, 0)

        @pl.when(t < Q)
        def _():
            fields(t)

        stage(RESIDUAL, WALL_TICKS[0], chord_stage)
        stage(TOTAL, WALL_TICKS[1], totals)
        stage(CARRY, WALL_TICKS[2], carried)
        stage(INNER_AHEAD, WALL_TICKS[3], inner_forward, inner)
        stage(INNER_BACK, WALL_TICKS[4], inner_back, inner)
        stage(OUTER_BACK, WALL_TICKS[5], outer_back, outer_dev)

        @pl.when(t == LOAD_PART)
        def _():
            load_parts()

        @pl.when(t == LOAD_SUM)
        def _():
            load_sums()

        return c

    lax.fori_loop(1, Q + OUTER_BACK, tick, 0)

    for copy in (wall_up(), wall_down()):
        copy.wait_send()

    def drain(i, c):
        @pl.when(i > 0)
        def _():
            fringe_up(i).wait_send()
            fringe_down(i).wait_send()
            low_up(i).wait_send()
            low_down(i).wait_send()
            outer_up(i).wait_send()
            outer_down(i).wait_send()
            out_copy(i).wait()

        chord_up(i).wait_send()
        chord_down(i).wait_send()
        for d in range(1, GROUP):
            group_send(i, d).wait_send()
        for d in range(1, groups):
            total_send(i, d).wait_send()

        @pl.when(inner)
        def _():
            a_copy(i).wait_send()
            x_copy(i).wait_send()

        @pl.when(outer_dev)
        def _():
            y_copy(i).wait_send()

        return c

    lax.fori_loop(0, Q, drain, 0)
    for d in range(1, SPANS):
        load_span(d).wait_send()

    def load_end(d, acc):
        load_wrap(d).wait()
        return acc + lrb[d - 1]

    final = lax.fori_loop(1, WRAPS, load_end, ld[wrap])
    loads[0] = final[0:3, 0:each]


def local(state, state_old, wrap_rate, span_rate, blank, section):
    def vm(*shape):
        return pltpu.VMEM(shape, jnp.float32)

    def im(*shape):
        return pltpu.VMEM(shape, jnp.int32)

    dma = pltpu.SemaphoreType.DMA
    scratch = [
        vm(Q, S, W, N), vm(Q, S, W, N), vm(Q, S, N), vm(Q, W, N), im(S, W, N // 2), im(S, H, N), im(S, W),
        vm(Q, S, H, N), vm(Q, S, H, N), vm(Q, S, H, N), vm(Q, S, H, N), vm(Q, S, H, N), vm(Q, S, W + 16, N),
        vm(Q, 2, W, N), vm(Q, 2, W, N), vm(Q, 2, H, N), vm(Q, 2, H, N), vm(Q, 2, H, N), vm(Q, 2, H, N),
        vm(Q, 8, N), vm(Q, 8, N), vm(Q, 8, N), vm(Q, 8, N), vm(Q, S, W, N),
        vm(Q, S, W + 8, N), vm(Q, S, W + 8, N), vm(Q, S, W + 8, N), vm(Q, S, W + 8, N), vm(Q, S, 16, N),
        vm(8, N), vm(Q, 8, 8, N), vm(Q, 2, 8, N), vm(Q, GROUP, 2, 8, N), vm(Q, 2, 8, N), vm(Q, WRAPS // GROUP, 2, 8, N),
        vm(2, 8, N), vm(Q, S, W, N), vm(Q, 9, W, N), vm(Q, 10, W, N), vm(Q, 8, W, N), vm(Q, W, N), vm(Q, W, N),
        vm(Q, 2, W, N), vm(Q, 2, W, N), vm(Q, 2, W, N), vm(Q, 2, W, N), vm(Q, 2, W, N), vm(Q, 2, W, N),
        vm(Q, S, W, N), vm(SPANS, 8, 256), vm(SPANS - 1, 8, 256), vm(WRAPS, 8, N), vm(WRAPS - 1, 8, N),
        dma((5,)), dma((V,)), dma((Q,)), dma((2, Q)), dma((2, Q)), dma((2,)), dma((2,)), dma((2, Q)), dma((2, Q)),
        dma((2, Q)), dma((2, Q)), dma((2, Q)), dma((2, Q)),
        dma((Q, GROUP - 1)), dma((Q, GROUP - 1)), dma((Q, 3)), dma((Q, 3)),
        dma((Q,)), dma((Q,)), dma((Q,)), dma((Q,)), dma((Q,)), dma((Q,)),
        dma((SPANS - 1,)), dma((SPANS - 1,)), dma((WRAPS - 1,)), dma((WRAPS - 1,)),
    ]
    each = SECTIONS // (SPANS * WRAPS)
    return pl.pallas_call(
        kernel,
        out_shape=(
            jax.ShapeDtypeStruct(state.shape, jnp.float32),
            jax.ShapeDtypeStruct((1, 3, each), jnp.float32),
        ),
        in_specs=[pl.BlockSpec(memory_space=pltpu.HBM)] * 6,
        out_specs=(pl.BlockSpec(memory_space=pltpu.HBM), pl.BlockSpec(memory_space=pltpu.VMEM)),
        scratch_shapes=scratch,
        compiler_params=pltpu.CompilerParams(
            collective_id=0, has_side_effects=True, vmem_limit_bytes=66_000_000),
    )(state, state_old, wrap_rate, span_rate, blank, section)


def solution(mesh):
    return jax.shard_map(
        local,
        mesh=mesh,
        in_specs=(
            P("blade", None, "span", "wrap", None),
            P("blade", None, "span", "wrap", None),
            P("blade", None, "span", None),
            P("blade", None, "wrap", None),
            P("blade", "span", "wrap", None),
            P("blade", "span", "wrap"),
        ),
        out_specs=(P("blade", None, "span", "wrap", None), P("blade", None, ("span", "wrap"))),
        check_vma=False,
    )
```

```python
import jax
import jax.numpy as jnp
from jax import lax
from jax.experimental import pallas as pl
from jax.experimental.pallas import tpu as pltpu
from jax.sharding import PartitionSpec as P

MESH = pl.DeviceIdType.MESH
SECTIONS = 640
V, S, W, N = 5, 4, 64, 128
Q = V + 1
H = W // 2
GROUP = 4
SPANS, WRAPS, BLADES = 4, 16, 4
LEVELS = 6


def line_roots(r):
    ri = 1.0 / r
    y = 6.0 + ri + jnp.sqrt(ri * (12.0 + ri))
    q = 2.0 / ((y - 2.0) + jnp.sqrt(y * (y - 4.0)))
    p = 6.0 * q / (1.0 + q)
    return p, q


def square(m):
    a, b, c, d = m
    bc = b * c
    tr = a + d
    return a * a + bc, b * tr, c * tr, d * d + bc


RESIDUAL, TOTAL, CARRY, INNER_AHEAD, INNER_BACK, OUTER_BACK = 3, 5, 8, 10, 12, 14
WALL_TICKS = (1, 3, 5, 7, 9, 11)
LOAD_PART, LOAD_SUM = 12, 14


def kernel(
    state, old, wrate, srate, blank, section,
    out, loads,
    st, so, wr, sr, bl, mk, sec, pk, lk, op, fb, fa, fl, hlo, hhi, llo, lhi, olo, ohi, cslo, cshi, crlo, crhi, fr,
    ga, gd, ub, ud, cf, r8, tm, ms, m1, gs, m2, cc, xb, l1t, l2t, rdt, alt, bet,
    ysend, yrecv, asend, arecv, xsend, xrecv, ob, la, lra, ld, lrb,
    in_s, st_s, fs, fq, hs, hq, ls, lq, os_, oq, cs, cq, r1s, r1q, r2s, r2q, ys, yq, as_, aq, xs, xq,
    las, laq, lbs, lbq,
):
    span = lax.axis_index("span")
    wrap = lax.axis_index("wrap")
    blade = lax.axis_index("blade")
    place = wrap % GROUP
    group = wrap // GROUP
    groups = WRAPS // GROUP

    barrier = pltpu.get_barrier_semaphore()
    for d in range(1, WRAPS):
        pl.semaphore_signal(barrier, inc=1, device_id={"wrap": (wrap + d) % WRAPS}, device_id_type=MESH)
    for d in range(1, SPANS):
        pl.semaphore_signal(barrier, inc=1, device_id={"span": (span + d) % SPANS}, device_id_type=MESH)
    for d in (1, BLADES - 1):
        pl.semaphore_signal(barrier, inc=1, device_id={"blade": (blade + d) % BLADES}, device_id_type=MESH)

    copy_wr = pltpu.make_async_copy(wrate.at[0], wr.at[1:Q], in_s.at[0])
    copy_st = [pltpu.make_async_copy(state.at[0, v], st.at[v + 1], st_s.at[v]) for v in range(V)]
    copy_bl = pltpu.make_async_copy(blank.at[0], bl, in_s.at[1])
    copy_sr = pltpu.make_async_copy(srate.at[0], sr.at[1:Q], in_s.at[2])
    copy_so = pltpu.make_async_copy(old.at[0], so.at[1:Q], in_s.at[3])
    copy_sec = pltpu.make_async_copy(section.at[0], sec, in_s.at[4])
    for copy in [copy_wr] + copy_st + [copy_bl, copy_sr, copy_so, copy_sec]:
        copy.start()

    lane_h = lax.broadcasted_iota(jnp.int32, (H, N), 1)
    lane_w = lax.broadcasted_iota(jnp.int32, (W, N), 1)
    row_w = lax.broadcasted_iota(jnp.int32, (W, N), 0)
    row_8 = lax.broadcasted_iota(jnp.int32, (8, N), 0)

    def wall_lanes(a, b, c, rest):
        lane = lax.broadcasted_iota(jnp.int32, a.shape, 1)
        return jnp.where(
            lane < 4, a, jnp.where(lane < 8, pltpu.roll(b, 4, 1), jnp.where(lane < 12, pltpu.roll(c, 8, 1), rest)))

    copy_wr.wait()
    wr[0] = wall_lanes(wr[2], wr[3], wr[4], 1.0)

    def chord_tables(idx, c):
        i = idx // S
        s = idx % S
        r = jnp.broadcast_to(wr[i, pl.ds(s, 1), :], (8, N))
        p, q = line_roots(r)
        g0 = (1.0 + q) * (2.0 * q) / (r * (1.0 - q) * (1.0 + q - p) * (1.0 + q + p))
        ratio = p / (1.0 + q)
        g1 = g0 * ratio
        pk_, qk_ = [p], [q]
        for k in range(LEVELS - 1):
            pk_.append(pk_[-1] * pk_[-1] - 2.0 * qk_[-1])
            qk_.append(qk_[-1] * qk_[-1])
        rows = pk_ + qk_ + [g0, -g1 * q, g1, -q * g0]

        def pick(values):
            tile = values[0]
            for n in range(1, 8):
                tile = jnp.where(row_8 == n, values[n], tile)
            return tile

        cf[i, s, 0:8, :] = pick(rows[0:8])
        cf[i, s, 8:16, :] = pick(rows[8:16])
        g = [g0, g1]
        for n in range(2, 17):
            g.append(p * g[-1] - q * g[-2])
        zero = jnp.zeros_like(p)
        u = [zero, zero + 1.0]
        for n in range(2, 17):
            u.append(p * u[-1] - q * u[-2])
        p3, q3 = pk_[3], qk_[3]

        def ascend(table, first, second):
            table[i, s, 0:8, :] = first
            table[i, s, 8:16, :] = second
            before, now = first, second
            for t in range(2, 9):
                before, now = now, p3 * now - q3 * before
                table[i, s, 8 * t : 8 * t + 8, :] = now

        def descend(table, last, first, second):
            table[i, s, 64:72, :] = last
            table[i, s, 56:64, :] = first
            table[i, s, 48:56, :] = second
            before, now = first, second
            for t in range(5, -1, -1):
                before, now = now, p3 * now - q3 * before
                table[i, s, 8 * t : 8 * t + 8, :] = now

        ascend(ga, pick(g[0:8]), pick(g[8:16]))
        descend(gd, jnp.where(row_8 == 0, g0, 0.0), pick(g[8:0:-1]), pick(g[16:8:-1]))
        ascend(ub, pick(u[0:8]), pick(u[8:16]))
        descend(ud, zero, pick(u[8:0:-1]), pick(u[16:8:-1]))
        return c

    lax.fori_loop(0, Q * S, chord_tables, 0)

    for copy in copy_st:
        copy.wait()

    def pack(i, c):
        for s in range(S):
            low = st[i, s, 0:H, :]
            high = st[i, s, H:W, :]
            pk[i, s] = jnp.where(lane_h < N // 2, pltpu.roll(low, N // 2, 1), high)
            lk[i, s] = jnp.where(lane_h < N // 2, low, pltpu.roll(high, N // 2, 1))
        return c

    lax.fori_loop(1, Q, pack, 0)

    for s in range(S):
        wall = wall_lanes(st[2, s], st[3, s], st[4, s], 0.0)
        fl[0, s, 8 : 8 + W, :] = wall
        cslo[0, 2 * s : 2 * s + 2, :] = wall[0:2]
        cshi[0, 2 * s : 2 * s + 2, :] = wall[W - 2 : W]

    def fringe_up(i):
        return pltpu.make_async_remote_copy(
            src_ref=pk.at[i], dst_ref=fb.at[i], send_sem=fs.at[0, i], recv_sem=fq.at[0, i],
            device_id={"blade": (blade + 1) % BLADES}, device_id_type=MESH)

    def fringe_down(i):
        return pltpu.make_async_remote_copy(
            src_ref=pk.at[i], dst_ref=fa.at[i], send_sem=fs.at[1, i], recv_sem=fq.at[1, i],
            device_id={"blade": (blade + BLADES - 1) % BLADES}, device_id_type=MESH)

    above = (span + 1) % SPANS
    below = (span + SPANS - 1) % SPANS

    def wall_up():
        return pltpu.make_async_remote_copy(
            src_ref=fl.at[0, 2:4, 8 : 8 + W, :], dst_ref=hlo.at[0], send_sem=hs.at[0], recv_sem=hq.at[0],
            device_id={"span": above}, device_id_type=MESH)

    def wall_down():
        return pltpu.make_async_remote_copy(
            src_ref=fl.at[0, 0:2, 8 : 8 + W, :], dst_ref=hhi.at[0], send_sem=hs.at[1], recv_sem=hq.at[1],
            device_id={"span": below}, device_id_type=MESH)

    def low_up(i):
        return pltpu.make_async_remote_copy(
            src_ref=lk.at[i, 2:4], dst_ref=llo.at[i], send_sem=ls.at[0, i], recv_sem=lq.at[0, i],
            device_id={"span": above}, device_id_type=MESH)

    def low_down(i):
        return pltpu.make_async_remote_copy(
            src_ref=lk.at[i, 0:2], dst_ref=lhi.at[i], send_sem=ls.at[1, i], recv_sem=lq.at[1, i],
            device_id={"span": below}, device_id_type=MESH)

    def outer_up(i):
        return pltpu.make_async_remote_copy(
            src_ref=op.at[i, 2:4], dst_ref=olo.at[i], send_sem=os_.at[0, i], recv_sem=oq.at[0, i],
            device_id={"span": above}, device_id_type=MESH)

    def outer_down(i):
        return pltpu.make_async_remote_copy(
            src_ref=op.at[i, 0:2], dst_ref=ohi.at[i], send_sem=os_.at[1, i], recv_sem=oq.at[1, i],
            device_id={"span": below}, device_id_type=MESH)

    def chord_up(i):
        return pltpu.make_async_remote_copy(
            src_ref=cshi.at[i], dst_ref=crlo.at[i], send_sem=cs.at[0, i], recv_sem=cq.at[0, i],
            device_id={"wrap": (wrap + 1) % WRAPS}, device_id_type=MESH)

    def chord_down(i):
        return pltpu.make_async_remote_copy(
            src_ref=cslo.at[i], dst_ref=crhi.at[i], send_sem=cs.at[1, i], recv_sem=cq.at[1, i],
            device_id={"wrap": (wrap + WRAPS - 1) % WRAPS}, device_id_type=MESH)

    def group_send(i, d):
        target = group * GROUP + (place + d) % GROUP
        return pltpu.make_async_remote_copy(
            src_ref=ms.at[i], dst_ref=m1.at[i, place], send_sem=r1s.at[i, d - 1], recv_sem=r1q.at[i, d - 1],
            device_id={"wrap": target}, device_id_type=MESH)

    def total_send(i, d):
        peer = GROUP - 1 - place if d % 2 else place
        target = (group + d) % groups * GROUP + peer
        return pltpu.make_async_remote_copy(
            src_ref=gs.at[i], dst_ref=m2.at[i, group], send_sem=r2s.at[i, d - 1], recv_sem=r2q.at[i, d - 1],
            device_id={"wrap": target}, device_id_type=MESH)

    pl.semaphore_wait(barrier, 2 + SPANS - 1 + WRAPS - 1)

    def first_sends(i, c):
        fringe_up(i).start()
        fringe_down(i).start()
        low_up(i).start()
        low_down(i).start()
        return c

    wall_up().start()
    wall_down().start()
    chord_up(0).start()
    chord_down(0).start()
    lax.fori_loop(1, Q, first_sends, 0)

    for copy in (copy_bl, copy_sr, copy_so, copy_sec):
        copy.wait()

    for s in range(S):
        mk[s] = jnp.concatenate([bl[s, 0:H, :], bl[s, H:W, :]], axis=-1)
        so[0, s] = wall_lanes(so[2, s], so[3, s], so[4, s], 0.0)
    sr[0] = wall_lanes(sr[2], sr[3], sr[4], 1.0)

    def transfers(i, c):
        rate = wr[i]
        r8[0:S, :] = rate
        r8[S : 2 * S, :] = rate
        p, q = line_roots(r8[...])
        m = (p, -q, jnp.ones_like(p), jnp.zeros_like(p))
        for k in range(LEVELS):
            m = square(m)
        for k in range(4):
            tm[i, k] = m[k]
        m = square(square(m))
        for k in range(4):
            tm[i, 4 + k] = m[k]
        return c

    lax.fori_loop(0, Q, transfers, 0)

    def span_tables(idx, c):
        i = idx // 8
        rows = pl.ds(pl.multiple_of((idx % 8) * 8, 8), 8)
        r = sr[i, rows, :]
        centre = 1.0 + 5.0 * r
        first = -3.0 * r
        second = 0.5 * r
        zero = jnp.zeros_like(r)
        one_l, two_l, rd = [zero], [zero], [1.0 / centre]
        for j in range(1, 10):
            two = second * rd[j - 2] if j >= 2 else zero
            two_l.append(two)
            if j == 9:
                break
            top = first - second * one_l[j - 1]
            one = top * rd[j - 1]
            one_l.append(one)
            if j < 8:
                rd.append(1.0 / (centre - one * top - two * second))
        for j in range(9):
            l1t[i, j, rows, :] = one_l[j]
        for j in range(10):
            l2t[i, j, rows, :] = two_l[j]
        for j in range(8):
            rdt[i, j, rows, :] = rd[j]
        alpha = 1.0 - two_l[9] * two_l[8]
        beta = one_l[8] - two_l[9] * one_l[7]
        det = 1.0 / ((alpha - beta) * (alpha + beta))
        alt[i, rows, :] = alpha * det
        bet[i, rows, :] = beta * det
        return c

    lax.fori_loop(0, Q * 8, span_tables, 0)

    def fields(i):
        fringe_up(i).wait_recv()
        fringe_down(i).wait_recv()
        for s in range(S):
            marks = mk[s]
            op[i, s] = jnp.where(marks == 1, fb[i, s], jnp.where(marks == 2, fa[i, s], pk[i, s]))
        outer_up(i).start()
        outer_down(i).start()
        for s in range(S):
            outer = op[i, s]
            low = jnp.where(lane_h >= N // 2, pltpu.roll(outer, N // 2, 1), st[i, s, 0:H, :])
            high = jnp.where(lane_h >= N // 2, outer, st[i, s, H:W, :])
            fl[i, s, 8 : 8 + H, :] = low
            fl[i, s, 8 + H : 8 + W, :] = high
            cslo[i, 2 * s : 2 * s + 2, :] = low[0:2]
            cshi[i, 2 * s : 2 * s + 2, :] = high[H - 2 : H]
        chord_up(i).start()
        chord_down(i).start()

    has_low = jnp.where(span > 0, 1.0, 0.0)
    has_high = jnp.where(span < SPANS - 1, 1.0, 0.0)

    def residuals(i):
        chord_up(i).wait_recv()
        chord_down(i).wait_recv()

        @pl.when(i == 0)
        def _():
            wall_up().wait_recv()
            wall_down().wait_recv()

        @pl.when(i > 0)
        def _():
            low_up(i).wait_recv()
            low_down(i).wait_recv()
            outer_up(i).wait_recv()
            outer_down(i).wait_recv()
            for low, outer, whole in ((llo, olo, hlo), (lhi, ohi, hhi)):
                for k in range(2):
                    whole[i, k, 0:H, :] = jnp.where(lane_h < N // 2, low[i, k], pltpu.roll(outer[i, k], N // 2, 1))
                    whole[i, k, H:W, :] = jnp.where(lane_h < N // 2, pltpu.roll(low[i, k], N // 2, 1), outer[i, k])

        for s in range(S):
            fl[i, s, 6:8, :] = crlo[i, 2 * s : 2 * s + 2, :]
            fl[i, s, 8 + W : 10 + W, :] = crhi[i, 2 * s : 2 * s + 2, :]

        def station(t):
            if t < 0:
                return hlo[i, t + 2] * has_low
            if t >= S:
                return hhi[i, t - S] * has_high
            return fl[i, t, 8 : 8 + W, :]

        inside = (lane_w & jnp.where(i == 0, 3, N - 1)) > 0
        for s in range(S):
            own = fl[i, s, 8 : 8 + W, :]
            ahead = jnp.where(lane_w < N - 1, pltpu.roll(own, N - 1, 1), 0.0)
            behind = jnp.where(inside, pltpu.roll(own, 1, 1), 0.0)
            wide = fl[i, s, 10 : 10 + W, :] + fl[i, s, 6 : 6 + W, :] + station(s + 2) + station(s - 2)
            plus = fl[i, s, 9 : 9 + W, :] + station(s + 1)
            minus = fl[i, s, 7 : 7 + W, :] + station(s - 1)
            rhs = (so[i, s] - 2.1 * own) + 0.25 * (ahead + behind) - 0.05 * wide - 0.3 * plus + 0.7 * minus
            fr[i, s] = rhs
            ms[i, 0, s : s + 1, :] = jnp.sum(gd[i, s, 0:W, :] * rhs, axis=0, keepdims=True)
            ms[i, 1, s : s + 1, :] = jnp.sum(gd[i, s, 1 : 1 + W, :] * rhs, axis=0, keepdims=True)
            ms[i, 0, S + s : S + s + 1, :] = jnp.sum(ga[i, s, 1 : 1 + W, :] * rhs, axis=0, keepdims=True)
            ms[i, 1, S + s : S + s + 1, :] = jnp.sum(ga[i, s, 0:W, :] * rhs, axis=0, keepdims=True)
        m1[i, place] = ms[i]
        for d in range(1, GROUP):
            group_send(i, d).start()

    def down(x, n):
        if n % 8 == 0:
            return jnp.concatenate([jnp.zeros((n, N), jnp.float32), x[: W - n]], axis=0)
        return jnp.where(row_w >= n, pltpu.roll(x, n, 0), 0.0)

    def up(x, n):
        if n % 8 == 0:
            return jnp.concatenate([x[n:], jnp.zeros((n, N), jnp.float32)], axis=0)
        return jnp.where(row_w < W - n, pltpu.roll(x, W - n, 0), 0.0)

    def sweeps(i, s):
        rhs = fr[i, s]

        def coef(k):
            return cf[i, s, k : k + 1, :]

        ahead = coef(12) * rhs + coef(13) * down(rhs, 1)
        back = coef(14) * up(rhs, 1) + coef(15) * up(rhs, 2)
        for k in range(LEVELS):
            n = 1 << k
            pc, qc = coef(k), coef(LEVELS + k)
            if 2 * n < W:
                ahead = ahead + pc * down(ahead, n) + qc * down(ahead, 2 * n)
                back = back + pc * up(back, n) + qc * up(back, 2 * n)
            else:
                ahead = ahead + pc * down(ahead, n)
                back = back + pc * up(back, n)
        xb[i, s] = ahead + back

    forward = row_8 < S
    steps = jnp.where(forward, place, GROUP - 1 - place)
    zero_8 = jnp.zeros((8, N), jnp.float32)

    def advance(t, acc, x):
        return (t[0] * acc[0] + t[1] * acc[1] + x[0], t[2] * acc[0] + t[3] * acc[1] + x[1])

    def ordered(ref, i, a, b):
        return tuple(jnp.where(forward, ref[i, a, k], ref[i, b, k]) for k in range(2))

    def totals(i):
        for d in range(1, GROUP):
            group_send(i, d).wait_recv()
        t = [tm[i, k] for k in range(4)]
        acc = (zero_8, zero_8)
        for j in range(GROUP):
            acc = advance(t, acc, ordered(m1, i, j, GROUP - 1 - j))
        gs[i, 0] = acc[0]
        gs[i, 1] = acc[1]
        for d in range(1, groups):
            total_send(i, d).start()
        m2[i, group, 0] = acc[0]
        m2[i, group, 1] = acc[1]

    low_side = span < SPANS // 2
    inner = (span == 1) | (span == 2)
    outer_dev = (span == 0) | (span == SPANS - 1)
    mate = jnp.where(span % 2 == 0, span + 1, span - 1)

    def half(h):
        return pl.ds(pl.multiple_of(h * H, 8), H)

    def spot(j):
        return jnp.where(low_side, j, S - 1 - j)

    def y_copy(i, h):
        return pltpu.make_async_remote_copy(
            src_ref=ysend.at[i, h], dst_ref=yrecv.at[i, h], send_sem=ys.at[i, h], recv_sem=yq.at[i, h],
            device_id={"span": mate}, device_id_type=MESH)

    def a_copy(i, h):
        return pltpu.make_async_remote_copy(
            src_ref=asend.at[i, h], dst_ref=arecv.at[i, h], send_sem=as_.at[i, h], recv_sem=aq.at[i, h],
            device_id={"span": SPANS - 1 - span}, device_id_type=MESH)

    def x_copy(i, h):
        return pltpu.make_async_remote_copy(
            src_ref=xsend.at[i, h], dst_ref=xrecv.at[i, h], send_sem=xs.at[i, h], recv_sem=xq.at[i, h],
            device_id={"span": mate}, device_id_type=MESH)

    def carried(i):
        for d in range(1, groups):
            total_send(i, d).wait_recv()
        t = [tm[i, k] for k in range(4)]
        t4 = [tm[i, 4 + k] for k in range(4)]
        acc = (zero_8, zero_8)
        for turn in range(2):
            for d in range(groups, 0, -1):
                acc = advance(t4, acc, ordered(m2, i, (group + groups - d) % groups, (group + d) % groups))
        for j in range(GROUP - 1):
            nxt = advance(t, acc, ordered(m1, i, j, GROUP - 1 - j))
            acc = tuple(jnp.where(j < steps, b, a) for a, b in zip(acc, nxt))
        cc[0] = acc[0]
        cc[1] = acc[1]
        for s in range(S):
            minus_q = -cf[i, s, LEVELS : LEVELS + 1, :]
            xb[i, s] = (
                xb[i, s]
                + ub[i, s, 1 : 1 + W, :] * cc[0, s : s + 1, :]
                + ub[i, s, 0:W, :] * (minus_q * cc[1, s : s + 1, :])
                + ud[i, s, 0:W, :] * cc[0, S + s : S + s + 1, :]
                + ud[i, s, 1 : 1 + W, :] * (minus_q * cc[1, S + s : S + s + 1, :])
            )

        @pl.when(outer_dev)
        def _():
            def part(h, c):
                rows = half(h)
                y = []
                for j in range(S):
                    now = xb[i, spot(j), rows, :]
                    if j >= 1:
                        now = now - l1t[i, j, rows, :] * y[j - 1]
                    if j >= 2:
                        now = now - l2t[i, j, rows, :] * y[j - 2]
                    y.append(now)
                    xb[i, spot(j), rows, :] = now * rdt[i, j, rows, :]
                ysend[i, h, 0] = y[S - 2]
                ysend[i, h, 1] = y[S - 1]
                y_copy(i, h).start()
                return c

            lax.fori_loop(0, 2, part, 0)

    def inner_forward(i):
        def part(h, c):
            rows = half(h)
            y_copy(i, h).wait_recv()
            y = [yrecv[i, h, 0], yrecv[i, h, 1]]
            for j in range(S):
                now = xb[i, spot(j), rows, :] - l1t[i, S + j, rows, :] * y[-1] - l2t[i, S + j, rows, :] * y[-2]
                y.append(now)
                scaled = now * rdt[i, S + j, rows, :]
                xb[i, spot(j), rows, :] = scaled
                if j >= S - 2:
                    asend[i, h, j - (S - 2)] = scaled
            a_copy(i, h).start()
            return c

        lax.fori_loop(0, 2, part, 0)

    def finish(i, h, xs_):
        rows = half(h)
        own = pl.ds(pl.multiple_of(8 + h * H, 8), H)
        spots_ = [spot(j) for j in range(S)]
        done = [fl[i, at, own, :] + x for at, x in zip(spots_, xs_)]

        @pl.when(i > 0)
        def _():
            for at, value in zip(spots_, done):
                out[0, i - 1, at, rows, :] = value

        @pl.when(i == 0)
        def _():
            for at, value in zip(spots_, done):
                ob[at, rows, :] = value

    def inner_back(i):
        def part(h, c):
            rows = half(h)

            def one(j):
                return l1t[i, j, rows, :]

            def two(j):
                return l2t[i, j, rows, :]

            a_copy(i, h).wait_recv()
            a6, a7 = xb[i, spot(2), rows, :], xb[i, spot(3), rows, :]
            b6, b7 = arecv[i, h, 0], arecv[i, h, 1]
            lead = a7 - two(9) * b6
            other = b7 - two(9) * a6
            x7 = alt[i, rows, :] * lead - bet[i, rows, :] * other
            x8 = alt[i, rows, :] * other - bet[i, rows, :] * lead
            x6 = a6 - one(7) * x7 - two(8) * x8
            x5 = xb[i, spot(1), rows, :] - one(6) * x6 - two(7) * x7
            x4 = xb[i, spot(0), rows, :] - one(5) * x5 - two(6) * x6
            xsend[i, h, 0] = x4
            xsend[i, h, 1] = x5
            x_copy(i, h).start()
            finish(i, h, (x4, x5, x6, x7))
            return c

        lax.fori_loop(0, 2, part, 0)

    def outer_back(i):
        def part(h, c):
            rows = half(h)
            x_copy(i, h).wait_recv()
            x = [xrecv[i, h, 1], xrecv[i, h, 0]]
            for j in range(S - 1, -1, -1):
                x.append(xb[i, spot(j), rows, :] - l1t[i, j + 1, rows, :] * x[-1] - l2t[i, j + 2, rows, :] * x[-2])
            finish(i, h, x[:1:-1])
            return c

        lax.fori_loop(0, 2, part, 0)

    part = SECTIONS // SPANS
    padded = 256
    each = part // WRAPS

    def load_span(d):
        return pltpu.make_async_remote_copy(
            src_ref=la.at[(span + d) % SPANS], dst_ref=lra.at[d - 1], send_sem=las.at[d - 1], recv_sem=laq.at[d - 1],
            device_id={"span": (span + d) % SPANS}, device_id_type=MESH)

    def load_wrap(d):
        target = (wrap + d) % WRAPS
        return pltpu.make_async_remote_copy(
            src_ref=ld.at[target], dst_ref=lrb.at[d - 1], send_sem=lbs.at[d - 1], recv_sem=lbq.at[d - 1],
            device_id={"wrap": target}, device_id_type=MESH)

    def load_parts():
        walls, names = [], []
        for s in range(S):
            value = ob[s]
            step = pltpu.roll(value, N - 1, 1) - value
            wall = jnp.where(
                lane_w == 0, step, jnp.where(
                    lane_w == 1, pltpu.roll(step, N - 3, 1), jnp.where(
                        lane_w == 2, pltpu.roll(step, N - 6, 1), 0.0)))
            walls.append(jnp.transpose(wall)[0:8, :])
            name = sec[s : s + 1, :]
            for k in range(1, SPANS):
                name = name + jnp.where(sec[s : s + 1, :] >= k * part, padded - part, 0)
            names.append(name)
        nodes = jnp.concatenate(walls, axis=1)
        spots = lax.broadcasted_iota(jnp.int32, (SPANS * padded, S * W), 0)
        picks = jnp.where(spots == jnp.concatenate(names, axis=1), 1.0, 0.0).astype(jnp.bfloat16)
        parts = []
        for k in range(3):
            piece = nodes.astype(jnp.bfloat16)
            nodes = nodes - piece.astype(jnp.float32)
            parts.append(piece.astype(jnp.float32))
        stacked = jnp.concatenate(parts + [jnp.zeros_like(nodes)], axis=0).astype(jnp.bfloat16)
        sums = lax.dot_general(
            stacked, picks, (((1,), (1,)), ((), ())), preferred_element_type=jnp.float32)
        total = sums[0:8] + sums[8:16] + sums[16:24]
        for k in range(SPANS):
            la[k] = total[:, k * padded : (k + 1) * padded]
        for d in range(1, SPANS):
            load_span(d).start()

    def load_sums():
        for d in range(1, SPANS):
            load_span(d).wait_recv()
        mine = la[span]
        for d in range(1, SPANS):
            mine = mine + lra[d - 1]
        for k in range(WRAPS):
            ld[k] = (mine if k == 0 else pltpu.roll(mine, padded - each * k, 1))[:, 0:N]

        def load_start(d, c):
            load_wrap(d).start()
            return c

        lax.fori_loop(1, WRAPS, load_start, 0)

    def tick(t, c):
        def stage(offset, wall, body, role=True):
            i = jnp.where(t == wall, 0, t - offset)

            @pl.when(((t == wall) | ((i >= 1) & (i < Q))) & role)
            def _():
                body(i)

        def chord_stage(i):
            residuals(i)

            def one(s, c):
                sweeps(i, s)
                return c

            lax.fori_loop(0, S, one, 0)

        @pl.when(t < Q)
        def _():
            fields(t)

        stage(RESIDUAL, WALL_TICKS[0], chord_stage)
        stage(TOTAL, WALL_TICKS[1], totals)
        stage(CARRY, WALL_TICKS[2], carried)
        stage(INNER_AHEAD, WALL_TICKS[3], inner_forward, inner)
        stage(INNER_BACK, WALL_TICKS[4], inner_back, inner)
        stage(OUTER_BACK, WALL_TICKS[5], outer_back, outer_dev)

        @pl.when(t == LOAD_PART)
        def _():
            load_parts()

        @pl.when(t == LOAD_SUM)
        def _():
            load_sums()

        return c

    lax.fori_loop(1, Q + OUTER_BACK, tick, 0)

    for copy in (wall_up(), wall_down()):
        copy.wait_send()

    def drain(i, c):
        @pl.when(i > 0)
        def _():
            fringe_up(i).wait_send()
            fringe_down(i).wait_send()
            low_up(i).wait_send()
            low_down(i).wait_send()
            outer_up(i).wait_send()
            outer_down(i).wait_send()

        chord_up(i).wait_send()
        chord_down(i).wait_send()
        for d in range(1, GROUP):
            group_send(i, d).wait_send()
        for d in range(1, groups):
            total_send(i, d).wait_send()

        @pl.when(inner)
        def _():
            for h in range(2):
                a_copy(i, h).wait_send()
                x_copy(i, h).wait_send()

        @pl.when(outer_dev)
        def _():
            for h in range(2):
                y_copy(i, h).wait_send()

        return c

    lax.fori_loop(0, Q, drain, 0)
    for d in range(1, SPANS):
        load_span(d).wait_send()

    def load_end(d, acc):
        load_wrap(d).wait()
        return acc + lrb[d - 1]

    final = lax.fori_loop(1, WRAPS, load_end, ld[wrap])
    for k in range(3):
        loads[k] = final[k : k + 1, 0:each]


def local(state, state_old, wrap_rate, span_rate, blank, section):
    def vm(*shape):
        return pltpu.VMEM(shape, jnp.float32)

    def im(*shape):
        return pltpu.VMEM(shape, jnp.int32)

    dma = pltpu.SemaphoreType.DMA
    scratch = [
        vm(Q, S, W, N), vm(Q, S, W, N), vm(Q, S, N), vm(Q, W, N), im(S, W, N // 2), im(S, H, N), im(S, W),
        vm(Q, S, H, N), vm(Q, S, H, N), vm(Q, S, H, N), vm(Q, S, H, N), vm(Q, S, H, N), vm(Q, S, W + 16, N),
        vm(Q, 2, W, N), vm(Q, 2, W, N), vm(Q, 2, H, N), vm(Q, 2, H, N), vm(Q, 2, H, N), vm(Q, 2, H, N),
        vm(Q, 8, N), vm(Q, 8, N), vm(Q, 8, N), vm(Q, 8, N), vm(Q, S, W, N),
        vm(Q, S, W + 8, N), vm(Q, S, W + 8, N), vm(Q, S, W + 8, N), vm(Q, S, W + 8, N), vm(Q, S, 16, N),
        vm(8, N), vm(Q, 8, 8, N), vm(Q, 2, 8, N), vm(Q, GROUP, 2, 8, N), vm(Q, 2, 8, N), vm(Q, WRAPS // GROUP, 2, 8, N),
        vm(2, 8, N), vm(Q, S, W, N), vm(Q, 9, W, N), vm(Q, 10, W, N), vm(Q, 8, W, N), vm(Q, W, N), vm(Q, W, N),
        vm(Q, 2, 2, H, N), vm(Q, 2, 2, H, N), vm(Q, 2, 2, H, N), vm(Q, 2, 2, H, N), vm(Q, 2, 2, H, N), vm(Q, 2, 2, H, N),
        vm(S, W, N), vm(SPANS, 8, 256), vm(SPANS - 1, 8, 256), vm(WRAPS, 8, N), vm(WRAPS - 1, 8, N),
        dma((5,)), dma((V,)), dma((2, Q)), dma((2, Q)), dma((2,)), dma((2,)), dma((2, Q)), dma((2, Q)),
        dma((2, Q)), dma((2, Q)), dma((2, Q)), dma((2, Q)),
        dma((Q, GROUP - 1)), dma((Q, GROUP - 1)), dma((Q, 3)), dma((Q, 3)),
        dma((Q, 2)), dma((Q, 2)), dma((Q, 2)), dma((Q, 2)), dma((Q, 2)), dma((Q, 2)),
        dma((SPANS - 1,)), dma((SPANS - 1,)), dma((WRAPS - 1,)), dma((WRAPS - 1,)),
    ]
    each = SECTIONS // (SPANS * WRAPS)
    updated, loads = pl.pallas_call(
        kernel,
        out_shape=(
            jax.ShapeDtypeStruct(state.shape, jnp.float32),
            jax.ShapeDtypeStruct((3, 1, each), jnp.float32),
        ),
        in_specs=[pl.BlockSpec(memory_space=pltpu.HBM)] * 6,
        out_specs=(pl.BlockSpec(memory_space=pltpu.VMEM), pl.BlockSpec(memory_space=pltpu.VMEM)),
        scratch_shapes=scratch,
        compiler_params=pltpu.CompilerParams(
            collective_id=0, has_side_effects=True, vmem_limit_bytes=50_000_000),
    )(*[pltpu.with_memory_space_constraint(a, pltpu.HBM) for a in (state, state_old, wrap_rate, span_rate, blank, section)])
    return updated, jnp.transpose(loads, (1, 0, 2))


def solution(mesh):
    return jax.shard_map(
        local,
        mesh=mesh,
        in_specs=(
            P("blade", None, "span", "wrap", None),
            P("blade", None, "span", "wrap", None),
            P("blade", None, "span", None),
            P("blade", None, "wrap", None),
            P("blade", "span", "wrap", None),
            P("blade", "span", "wrap"),
        ),
        out_specs=(P("blade", None, "span", "wrap", None), P("blade", None, ("span", "wrap"))),
        check_vma=False,
    )
```

```python
import jax
import jax.numpy as jnp
from jax import lax
from jax.experimental import pallas as pl
from jax.experimental.pallas import tpu as pltpu
from jax.sharding import PartitionSpec as P

MESH = pl.DeviceIdType.MESH
SECTIONS = 640
V, S, W, N = 5, 4, 64, 128
Q = V + 1
H = W // 2
GROUP = 8
SPANS, WRAPS, BLADES = 4, 16, 4
LEVELS = 6


def line_roots(r):
    ri = 1.0 / r
    y = 6.0 + ri + jnp.sqrt(ri * (12.0 + ri))
    q = 2.0 / ((y - 2.0) + jnp.sqrt(y * (y - 4.0)))
    p = 6.0 * q / (1.0 + q)
    return p, q


def square(m):
    a, b, c, d = m
    bc = b * c
    tr = a + d
    return a * a + bc, b * tr, c * tr, d * d + bc


RESIDUAL, TOTAL, CARRY, INNER_AHEAD, INNER_BACK, OUTER_BACK = 3, 6, 8, 10, 12, 14
WALL_TICKS = (1, 3, 5, 7, 9, 11)
LOAD_PART, LOAD_SUM = 12, 14


def kernel(
    state, old, wrate, srate, blank, section,
    out, loads,
    st, so, wr, sr, bl, mk, sec, pk, lk, op, fb, fa, fl, hlo, hhi, llo, lhi, olo, ohi, cslo, cshi, crlo, crhi, fr,
    ga, gd, ub, ud, cf, r8, tm, ms, m1, gs, m2, cc, xb, l1t, l2t, rdt, alt, bet,
    ysend, yrecv, asend, arecv, xsend, xrecv, ob, la, lra, ld, lrb,
    in_s, st_s, fs, fq, hs, hq, ls, lq, os_, oq, cs, cq, r1s, r1q, r2s, r2q, ys, yq, as_, aq, xs, xq,
    las, laq, lbs, lbq,
):
    span = lax.axis_index("span")
    wrap = lax.axis_index("wrap")
    blade = lax.axis_index("blade")
    place = wrap % GROUP
    group = wrap // GROUP
    groups = WRAPS // GROUP

    barrier = pltpu.get_barrier_semaphore()
    for d in range(1, WRAPS):
        pl.semaphore_signal(barrier, inc=1, device_id={"wrap": (wrap + d) % WRAPS}, device_id_type=MESH)
    for d in range(1, SPANS):
        pl.semaphore_signal(barrier, inc=1, device_id={"span": (span + d) % SPANS}, device_id_type=MESH)
    for d in (1, BLADES - 1):
        pl.semaphore_signal(barrier, inc=1, device_id={"blade": (blade + d) % BLADES}, device_id_type=MESH)

    copy_wr = pltpu.make_async_copy(wrate.at[0], wr.at[1:Q], in_s.at[0])
    copy_st = [pltpu.make_async_copy(state.at[0, v], st.at[v + 1], st_s.at[v]) for v in range(V)]
    copy_bl = pltpu.make_async_copy(blank.at[0], bl, in_s.at[1])
    copy_sr = pltpu.make_async_copy(srate.at[0], sr.at[1:Q], in_s.at[2])
    copy_so = pltpu.make_async_copy(old.at[0], so.at[1:Q], in_s.at[3])
    copy_sec = pltpu.make_async_copy(section.at[0], sec, in_s.at[4])
    for copy in [copy_wr] + copy_st + [copy_bl, copy_sr, copy_so, copy_sec]:
        copy.start()

    lane_h = lax.broadcasted_iota(jnp.int32, (H, N), 1)
    lane_w = lax.broadcasted_iota(jnp.int32, (W, N), 1)
    row_w = lax.broadcasted_iota(jnp.int32, (W, N), 0)
    row_8 = lax.broadcasted_iota(jnp.int32, (8, N), 0)

    def wall_lanes(a, b, c, rest):
        lane = lax.broadcasted_iota(jnp.int32, a.shape, 1)
        return jnp.where(
            lane < 4, a, jnp.where(lane < 8, pltpu.roll(b, 4, 1), jnp.where(lane < 12, pltpu.roll(c, 8, 1), rest)))

    copy_wr.wait()
    wr[0] = wall_lanes(wr[2], wr[3], wr[4], 1.0)

    def chord_tables(idx, c):
        i = idx // S
        s = idx % S
        r = jnp.broadcast_to(wr[i, pl.ds(s, 1), :], (8, N))
        p, q = line_roots(r)
        g0 = (1.0 + q) * (2.0 * q) / (r * (1.0 - q) * (1.0 + q - p) * (1.0 + q + p))
        ratio = p / (1.0 + q)
        g1 = g0 * ratio
        pk_, qk_ = [p], [q]
        for k in range(LEVELS - 1):
            pk_.append(pk_[-1] * pk_[-1] - 2.0 * qk_[-1])
            qk_.append(qk_[-1] * qk_[-1])
        rows = pk_ + qk_ + [g0, -g1 * q, g1, -q * g0]

        def pick(values):
            tile = values[0]
            for n in range(1, 8):
                tile = jnp.where(row_8 == n, values[n], tile)
            return tile

        cf[i, s, 0:8, :] = pick(rows[0:8])
        cf[i, s, 8:16, :] = pick(rows[8:16])
        g = [g0, g1]
        for n in range(2, 17):
            g.append(p * g[-1] - q * g[-2])
        zero = jnp.zeros_like(p)
        u = [zero, zero + 1.0]
        for n in range(2, 17):
            u.append(p * u[-1] - q * u[-2])
        p3, q3 = pk_[3], qk_[3]

        def ascend(table, first, second):
            table[i, s, 0:8, :] = first
            table[i, s, 8:16, :] = second
            before, now = first, second
            for t in range(2, 9):
                before, now = now, p3 * now - q3 * before
                table[i, s, 8 * t : 8 * t + 8, :] = now

        def descend(table, last, first, second):
            table[i, s, 64:72, :] = last
            table[i, s, 56:64, :] = first
            table[i, s, 48:56, :] = second
            before, now = first, second
            for t in range(5, -1, -1):
                before, now = now, p3 * now - q3 * before
                table[i, s, 8 * t : 8 * t + 8, :] = now

        ascend(ga, pick(g[0:8]), pick(g[8:16]))
        descend(gd, jnp.where(row_8 == 0, g0, 0.0), pick(g[8:0:-1]), pick(g[16:8:-1]))
        ascend(ub, pick(u[0:8]), pick(u[8:16]))
        descend(ud, zero, pick(u[8:0:-1]), pick(u[16:8:-1]))
        return c

    lax.fori_loop(0, Q * S, chord_tables, 0)

    for copy in copy_st:
        copy.wait()

    def pack(i, c):
        for s in range(S):
            low = st[i, s, 0:H, :]
            high = st[i, s, H:W, :]
            pk[i, s] = jnp.where(lane_h < N // 2, pltpu.roll(low, N // 2, 1), high)
            lk[i, s] = jnp.where(lane_h < N // 2, low, pltpu.roll(high, N // 2, 1))
        return c

    lax.fori_loop(1, Q, pack, 0)

    for s in range(S):
        wall = wall_lanes(st[2, s], st[3, s], st[4, s], 0.0)
        fl[0, s, 8 : 8 + W, :] = wall
        cslo[0, 2 * s : 2 * s + 2, :] = wall[0:2]
        cshi[0, 2 * s : 2 * s + 2, :] = wall[W - 2 : W]

    def fringe_up(i):
        return pltpu.make_async_remote_copy(
            src_ref=pk.at[i], dst_ref=fb.at[i], send_sem=fs.at[0, i], recv_sem=fq.at[0, i],
            device_id={"blade": (blade + 1) % BLADES}, device_id_type=MESH)

    def fringe_down(i):
        return pltpu.make_async_remote_copy(
            src_ref=pk.at[i], dst_ref=fa.at[i], send_sem=fs.at[1, i], recv_sem=fq.at[1, i],
            device_id={"blade": (blade + BLADES - 1) % BLADES}, device_id_type=MESH)

    above = (span + 1) % SPANS
    below = (span + SPANS - 1) % SPANS

    def wall_up():
        return pltpu.make_async_remote_copy(
            src_ref=fl.at[0, 2:4, 8 : 8 + W, :], dst_ref=hlo.at[0], send_sem=hs.at[0], recv_sem=hq.at[0],
            device_id={"span": above}, device_id_type=MESH)

    def wall_down():
        return pltpu.make_async_remote_copy(
            src_ref=fl.at[0, 0:2, 8 : 8 + W, :], dst_ref=hhi.at[0], send_sem=hs.at[1], recv_sem=hq.at[1],
            device_id={"span": below}, device_id_type=MESH)

    def low_up(i):
        return pltpu.make_async_remote_copy(
            src_ref=lk.at[i, 2:4], dst_ref=llo.at[i], send_sem=ls.at[0, i], recv_sem=lq.at[0, i],
            device_id={"span": above}, device_id_type=MESH)

    def low_down(i):
        return pltpu.make_async_remote_copy(
            src_ref=lk.at[i, 0:2], dst_ref=lhi.at[i], send_sem=ls.at[1, i], recv_sem=lq.at[1, i],
            device_id={"span": below}, device_id_type=MESH)

    def outer_up(i):
        return pltpu.make_async_remote_copy(
            src_ref=op.at[i, 2:4], dst_ref=olo.at[i], send_sem=os_.at[0, i], recv_sem=oq.at[0, i],
            device_id={"span": above}, device_id_type=MESH)

    def outer_down(i):
        return pltpu.make_async_remote_copy(
            src_ref=op.at[i, 0:2], dst_ref=ohi.at[i], send_sem=os_.at[1, i], recv_sem=oq.at[1, i],
            device_id={"span": below}, device_id_type=MESH)

    def chord_up(i):
        return pltpu.make_async_remote_copy(
            src_ref=cshi.at[i], dst_ref=crlo.at[i], send_sem=cs.at[0, i], recv_sem=cq.at[0, i],
            device_id={"wrap": (wrap + 1) % WRAPS}, device_id_type=MESH)

    def chord_down(i):
        return pltpu.make_async_remote_copy(
            src_ref=cslo.at[i], dst_ref=crhi.at[i], send_sem=cs.at[1, i], recv_sem=cq.at[1, i],
            device_id={"wrap": (wrap + WRAPS - 1) % WRAPS}, device_id_type=MESH)

    def group_send(i, d):
        target = group * GROUP + (place + d) % GROUP
        return pltpu.make_async_remote_copy(
            src_ref=ms.at[i], dst_ref=m1.at[i, place], send_sem=r1s.at[i, d - 1], recv_sem=r1q.at[i, d - 1],
            device_id={"wrap": target}, device_id_type=MESH)

    def total_send(i, d):
        target = (group + d) % groups * GROUP + place
        return pltpu.make_async_remote_copy(
            src_ref=gs.at[i], dst_ref=m2.at[i, group], send_sem=r2s.at[i, d - 1], recv_sem=r2q.at[i, d - 1],
            device_id={"wrap": target}, device_id_type=MESH)

    pl.semaphore_wait(barrier, 2 + SPANS - 1 + WRAPS - 1)

    def first_sends(i, c):
        fringe_up(i).start()
        fringe_down(i).start()
        low_up(i).start()
        low_down(i).start()
        return c

    wall_up().start()
    wall_down().start()
    chord_up(0).start()
    chord_down(0).start()
    lax.fori_loop(1, Q, first_sends, 0)

    for copy in (copy_bl, copy_sr, copy_so, copy_sec):
        copy.wait()

    for s in range(S):
        mk[s] = jnp.concatenate([bl[s, 0:H, :], bl[s, H:W, :]], axis=-1)
        so[0, s] = wall_lanes(so[2, s], so[3, s], so[4, s], 0.0)
    sr[0] = wall_lanes(sr[2], sr[3], sr[4], 1.0)

    def transfers(i, c):
        rate = wr[i]
        r8[0:S, :] = rate
        r8[S : 2 * S, :] = rate
        p, q = line_roots(r8[...])
        m = (p, -q, jnp.ones_like(p), jnp.zeros_like(p))
        for k in range(LEVELS):
            m = square(m)
        for k in range(4):
            tm[i, k] = m[k]
        m = square(square(square(m)))
        for k in range(4):
            tm[i, 4 + k] = m[k]
        return c

    lax.fori_loop(0, Q, transfers, 0)

    def span_tables(idx, c):
        i = idx // 8
        rows = pl.ds(pl.multiple_of((idx % 8) * 8, 8), 8)
        r = sr[i, rows, :]
        centre = 1.0 + 5.0 * r
        first = -3.0 * r
        second = 0.5 * r
        zero = jnp.zeros_like(r)
        one_l, two_l, rd = [zero], [zero], [1.0 / centre]
        for j in range(1, 10):
            two = second * rd[j - 2] if j >= 2 else zero
            two_l.append(two)
            if j == 9:
                break
            top = first - second * one_l[j - 1]
            one = top * rd[j - 1]
            one_l.append(one)
            if j < 8:
                rd.append(1.0 / (centre - one * top - two * second))
        for j in range(9):
            l1t[i, j, rows, :] = one_l[j]
        for j in range(10):
            l2t[i, j, rows, :] = two_l[j]
        for j in range(8):
            rdt[i, j, rows, :] = rd[j]
        alpha = 1.0 - two_l[9] * two_l[8]
        beta = one_l[8] - two_l[9] * one_l[7]
        det = 1.0 / ((alpha - beta) * (alpha + beta))
        alt[i, rows, :] = alpha * det
        bet[i, rows, :] = beta * det
        return c

    lax.fori_loop(0, Q * 8, span_tables, 0)

    def fields(i):
        fringe_up(i).wait_recv()
        fringe_down(i).wait_recv()
        for s in range(S):
            marks = mk[s]
            op[i, s] = jnp.where(marks == 1, fb[i, s], jnp.where(marks == 2, fa[i, s], pk[i, s]))
        outer_up(i).start()
        outer_down(i).start()
        for s in range(S):
            outer = op[i, s]
            low = jnp.where(lane_h >= N // 2, pltpu.roll(outer, N // 2, 1), st[i, s, 0:H, :])
            high = jnp.where(lane_h >= N // 2, outer, st[i, s, H:W, :])
            fl[i, s, 8 : 8 + H, :] = low
            fl[i, s, 8 + H : 8 + W, :] = high
            cslo[i, 2 * s : 2 * s + 2, :] = low[0:2]
            cshi[i, 2 * s : 2 * s + 2, :] = high[H - 2 : H]
        chord_up(i).start()
        chord_down(i).start()

    has_low = jnp.where(span > 0, 1.0, 0.0)
    has_high = jnp.where(span < SPANS - 1, 1.0, 0.0)

    def residuals(i):
        chord_up(i).wait_recv()
        chord_down(i).wait_recv()

        @pl.when(i == 0)
        def _():
            wall_up().wait_recv()
            wall_down().wait_recv()

        @pl.when(i > 0)
        def _():
            low_up(i).wait_recv()
            low_down(i).wait_recv()
            outer_up(i).wait_recv()
            outer_down(i).wait_recv()
            for low, outer, whole in ((llo, olo, hlo), (lhi, ohi, hhi)):
                for k in range(2):
                    whole[i, k, 0:H, :] = jnp.where(lane_h < N // 2, low[i, k], pltpu.roll(outer[i, k], N // 2, 1))
                    whole[i, k, H:W, :] = jnp.where(lane_h < N // 2, pltpu.roll(low[i, k], N // 2, 1), outer[i, k])

        for s in range(S):
            fl[i, s, 6:8, :] = crlo[i, 2 * s : 2 * s + 2, :]
            fl[i, s, 8 + W : 10 + W, :] = crhi[i, 2 * s : 2 * s + 2, :]

        def station(t):
            if t < 0:
                return hlo[i, t + 2] * has_low
            if t >= S:
                return hhi[i, t - S] * has_high
            return fl[i, t, 8 : 8 + W, :]

        inside = (lane_w & jnp.where(i == 0, 3, N - 1)) > 0
        for s in range(S):
            own = fl[i, s, 8 : 8 + W, :]
            ahead = jnp.where(lane_w < N - 1, pltpu.roll(own, N - 1, 1), 0.0)
            behind = jnp.where(inside, pltpu.roll(own, 1, 1), 0.0)
            wide = fl[i, s, 10 : 10 + W, :] + fl[i, s, 6 : 6 + W, :] + station(s + 2) + station(s - 2)
            plus = fl[i, s, 9 : 9 + W, :] + station(s + 1)
            minus = fl[i, s, 7 : 7 + W, :] + station(s - 1)
            rhs = (so[i, s] - 2.1 * own) + 0.25 * (ahead + behind) - 0.05 * wide - 0.3 * plus + 0.7 * minus
            fr[i, s] = rhs
            ms[i, 0, s : s + 1, :] = jnp.sum(gd[i, s, 0:W, :] * rhs, axis=0, keepdims=True)
            ms[i, 1, s : s + 1, :] = jnp.sum(gd[i, s, 1 : 1 + W, :] * rhs, axis=0, keepdims=True)
            ms[i, 0, S + s : S + s + 1, :] = jnp.sum(ga[i, s, 1 : 1 + W, :] * rhs, axis=0, keepdims=True)
            ms[i, 1, S + s : S + s + 1, :] = jnp.sum(ga[i, s, 0:W, :] * rhs, axis=0, keepdims=True)
        m1[i, place] = ms[i]
        for d in (4, 3, 5, 2, 6, 1, 7):
            group_send(i, d).start()

    def down(x, n):
        if n % 8 == 0:
            return jnp.concatenate([jnp.zeros((n, N), jnp.float32), x[: W - n]], axis=0)
        return jnp.where(row_w >= n, pltpu.roll(x, n, 0), 0.0)

    def up(x, n):
        if n % 8 == 0:
            return jnp.concatenate([x[n:], jnp.zeros((n, N), jnp.float32)], axis=0)
        return jnp.where(row_w < W - n, pltpu.roll(x, W - n, 0), 0.0)

    def sweeps(i, s):
        rhs = fr[i, s]

        def coef(k):
            return cf[i, s, k : k + 1, :]

        ahead = coef(12) * rhs + coef(13) * down(rhs, 1)
        back = coef(14) * up(rhs, 1) + coef(15) * up(rhs, 2)
        for k in range(LEVELS):
            n = 1 << k
            pc, qc = coef(k), coef(LEVELS + k)
            if 2 * n < W:
                ahead = ahead + pc * down(ahead, n) + qc * down(ahead, 2 * n)
                back = back + pc * up(back, n) + qc * up(back, 2 * n)
            else:
                ahead = ahead + pc * down(ahead, n)
                back = back + pc * up(back, n)
        xb[i, s] = ahead + back

    forward = row_8 < S
    steps = jnp.where(forward, place, GROUP - 1 - place)
    zero_8 = jnp.zeros((8, N), jnp.float32)

    def advance(t, acc, x):
        return (t[0] * acc[0] + t[1] * acc[1] + x[0], t[2] * acc[0] + t[3] * acc[1] + x[1])

    def ordered(ref, i, a, b):
        return tuple(jnp.where(forward, ref[i, a, k], ref[i, b, k]) for k in range(2))

    def totals(i):
        for d in range(1, GROUP):
            group_send(i, d).wait_recv()
        t = [tm[i, k] for k in range(4)]
        acc = (zero_8, zero_8)
        for j in range(GROUP):
            acc = advance(t, acc, ordered(m1, i, j, GROUP - 1 - j))
        gs[i, 0] = acc[0]
        gs[i, 1] = acc[1]
        for d in range(1, groups):
            total_send(i, d).start()
        m2[i, group, 0] = acc[0]
        m2[i, group, 1] = acc[1]

    low_side = span < SPANS // 2
    inner = (span == 1) | (span == 2)
    outer_dev = (span == 0) | (span == SPANS - 1)
    mate = jnp.where(span % 2 == 0, span + 1, span - 1)

    def half(h):
        return pl.ds(pl.multiple_of(h * H, 8), H)

    def spot(j):
        return jnp.where(low_side, j, S - 1 - j)

    def y_copy(i, h):
        return pltpu.make_async_remote_copy(
            src_ref=ysend.at[i, h], dst_ref=yrecv.at[i, h], send_sem=ys.at[i, h], recv_sem=yq.at[i, h],
            device_id={"span": mate}, device_id_type=MESH)

    def a_copy(i, h):
        return pltpu.make_async_remote_copy(
            src_ref=asend.at[i, h], dst_ref=arecv.at[i, h], send_sem=as_.at[i, h], recv_sem=aq.at[i, h],
            device_id={"span": SPANS - 1 - span}, device_id_type=MESH)

    def x_copy(i, h):
        return pltpu.make_async_remote_copy(
            src_ref=xsend.at[i, h], dst_ref=xrecv.at[i, h], send_sem=xs.at[i, h], recv_sem=xq.at[i, h],
            device_id={"span": mate}, device_id_type=MESH)

    def carried(i):
        for d in range(1, groups):
            total_send(i, d).wait_recv()
        t = [tm[i, k] for k in range(4)]
        t4 = [tm[i, 4 + k] for k in range(4)]
        acc = (zero_8, zero_8)
        for turn in range(2):
            for d in range(groups, 0, -1):
                acc = advance(t4, acc, ordered(m2, i, (group + groups - d) % groups, (group + d) % groups))
        for j in range(GROUP - 1):
            nxt = advance(t, acc, ordered(m1, i, j, GROUP - 1 - j))
            acc = tuple(jnp.where(j < steps, b, a) for a, b in zip(acc, nxt))
        cc[0] = acc[0]
        cc[1] = acc[1]
        for s in range(S):
            minus_q = -cf[i, s, LEVELS : LEVELS + 1, :]
            xb[i, s] = (
                xb[i, s]
                + ub[i, s, 1 : 1 + W, :] * cc[0, s : s + 1, :]
                + ub[i, s, 0:W, :] * (minus_q * cc[1, s : s + 1, :])
                + ud[i, s, 0:W, :] * cc[0, S + s : S + s + 1, :]
                + ud[i, s, 1 : 1 + W, :] * (minus_q * cc[1, S + s : S + s + 1, :])
            )

        @pl.when(outer_dev)
        def _():
            def part(h, c):
                rows = half(h)
                y = []
                for j in range(S):
                    now = xb[i, spot(j), rows, :]
                    if j >= 1:
                        now = now - l1t[i, j, rows, :] * y[j - 1]
                    if j >= 2:
                        now = now - l2t[i, j, rows, :] * y[j - 2]
                    y.append(now)
                    xb[i, spot(j), rows, :] = now * rdt[i, j, rows, :]
                ysend[i, h, 0] = y[S - 2]
                ysend[i, h, 1] = y[S - 1]
                y_copy(i, h).start()
                return c

            lax.fori_loop(0, 2, part, 0)

    def inner_forward(i):
        def part(h, c):
            rows = half(h)
            y_copy(i, h).wait_recv()
            y = [yrecv[i, h, 0], yrecv[i, h, 1]]
            for j in range(S):
                now = xb[i, spot(j), rows, :] - l1t[i, S + j, rows, :] * y[-1] - l2t[i, S + j, rows, :] * y[-2]
                y.append(now)
                scaled = now * rdt[i, S + j, rows, :]
                xb[i, spot(j), rows, :] = scaled
                if j >= S - 2:
                    asend[i, h, j - (S - 2)] = scaled
            a_copy(i, h).start()
            return c

        lax.fori_loop(0, 2, part, 0)

    def finish(i, h, xs_):
        rows = half(h)
        own = pl.ds(pl.multiple_of(8 + h * H, 8), H)
        spots_ = [spot(j) for j in range(S)]
        done = [fl[i, at, own, :] + x for at, x in zip(spots_, xs_)]

        @pl.when(i > 0)
        def _():
            for at, value in zip(spots_, done):
                out[0, i - 1, at, rows, :] = value

        @pl.when(i == 0)
        def _():
            for at, value in zip(spots_, done):
                ob[at, rows, :] = value

    def inner_back(i):
        def part(h, c):
            rows = half(h)

            def one(j):
                return l1t[i, j, rows, :]

            def two(j):
                return l2t[i, j, rows, :]

            a_copy(i, h).wait_recv()
            a6, a7 = xb[i, spot(2), rows, :], xb[i, spot(3), rows, :]
            b6, b7 = arecv[i, h, 0], arecv[i, h, 1]
            lead = a7 - two(9) * b6
            other = b7 - two(9) * a6
            x7 = alt[i, rows, :] * lead - bet[i, rows, :] * other
            x8 = alt[i, rows, :] * other - bet[i, rows, :] * lead
            x6 = a6 - one(7) * x7 - two(8) * x8
            x5 = xb[i, spot(1), rows, :] - one(6) * x6 - two(7) * x7
            x4 = xb[i, spot(0), rows, :] - one(5) * x5 - two(6) * x6
            xsend[i, h, 0] = x4
            xsend[i, h, 1] = x5
            x_copy(i, h).start()
            finish(i, h, (x4, x5, x6, x7))
            return c

        lax.fori_loop(0, 2, part, 0)

    def outer_back(i):
        def part(h, c):
            rows = half(h)
            x_copy(i, h).wait_recv()
            x = [xrecv[i, h, 1], xrecv[i, h, 0]]
            for j in range(S - 1, -1, -1):
                x.append(xb[i, spot(j), rows, :] - l1t[i, j + 1, rows, :] * x[-1] - l2t[i, j + 2, rows, :] * x[-2])
            finish(i, h, x[:1:-1])
            return c

        lax.fori_loop(0, 2, part, 0)

    part = SECTIONS // SPANS
    padded = 256
    each = part // WRAPS

    def load_span(d):
        return pltpu.make_async_remote_copy(
            src_ref=la.at[(span + d) % SPANS], dst_ref=lra.at[d - 1], send_sem=las.at[d - 1], recv_sem=laq.at[d - 1],
            device_id={"span": (span + d) % SPANS}, device_id_type=MESH)

    def load_wrap(d):
        target = (wrap + d) % WRAPS
        return pltpu.make_async_remote_copy(
            src_ref=ld.at[target], dst_ref=lrb.at[d - 1], send_sem=lbs.at[d - 1], recv_sem=lbq.at[d - 1],
            device_id={"wrap": target}, device_id_type=MESH)

    def load_parts():
        walls, names = [], []
        for s in range(S):
            value = ob[s]
            step = pltpu.roll(value, N - 1, 1) - value
            wall = jnp.where(
                lane_w == 0, step, jnp.where(
                    lane_w == 1, pltpu.roll(step, N - 3, 1), jnp.where(
                        lane_w == 2, pltpu.roll(step, N - 6, 1), 0.0)))
            walls.append(jnp.transpose(wall)[0:8, :])
            name = sec[s : s + 1, :]
            for k in range(1, SPANS):
                name = name + jnp.where(sec[s : s + 1, :] >= k * part, padded - part, 0)
            names.append(name)
        nodes = jnp.concatenate(walls, axis=1)
        spots = lax.broadcasted_iota(jnp.int32, (SPANS * padded, S * W), 0)
        picks = jnp.where(spots == jnp.concatenate(names, axis=1), 1.0, 0.0).astype(jnp.bfloat16)
        parts = []
        for k in range(3):
            piece = nodes.astype(jnp.bfloat16)
            nodes = nodes - piece.astype(jnp.float32)
            parts.append(piece.astype(jnp.float32))
        stacked = jnp.concatenate(parts + [jnp.zeros_like(nodes)], axis=0).astype(jnp.bfloat16)
        sums = lax.dot_general(
            stacked, picks, (((1,), (1,)), ((), ())), preferred_element_type=jnp.float32)
        total = sums[0:8] + sums[8:16] + sums[16:24]
        for k in range(SPANS):
            la[k] = total[:, k * padded : (k + 1) * padded]
        for d in range(1, SPANS):
            load_span(d).start()

    def load_sums():
        for d in range(1, SPANS):
            load_span(d).wait_recv()
        mine = la[span]
        for d in range(1, SPANS):
            mine = mine + lra[d - 1]
        for k in range(WRAPS):
            ld[k] = (mine if k == 0 else pltpu.roll(mine, padded - each * k, 1))[:, 0:N]

        def load_start(d, c):
            load_wrap(d).start()
            return c

        lax.fori_loop(1, WRAPS, load_start, 0)

    def tick(t, c):
        def stage(offset, wall, body, role=True):
            i = jnp.where(t == wall, 0, t - offset)

            @pl.when(((t == wall) | ((i >= 1) & (i < Q))) & role)
            def _():
                body(i)

        def chord_stage(i):
            residuals(i)

            def one(s, c):
                sweeps(i, s)
                return c

            lax.fori_loop(0, S, one, 0)

        @pl.when(t < Q)
        def _():
            fields(t)

        stage(RESIDUAL, WALL_TICKS[0], chord_stage)
        stage(TOTAL, WALL_TICKS[1], totals)
        stage(CARRY, WALL_TICKS[2], carried)
        stage(INNER_AHEAD, WALL_TICKS[3], inner_forward, inner)
        stage(INNER_BACK, WALL_TICKS[4], inner_back, inner)
        stage(OUTER_BACK, WALL_TICKS[5], outer_back, outer_dev)

        @pl.when(t == LOAD_PART)
        def _():
            load_parts()

        @pl.when(t == LOAD_SUM)
        def _():
            load_sums()

        return c

    lax.fori_loop(1, Q + OUTER_BACK, tick, 0)

    for copy in (wall_up(), wall_down()):
        copy.wait_send()

    def drain(i, c):
        @pl.when(i > 0)
        def _():
            fringe_up(i).wait_send()
            fringe_down(i).wait_send()
            low_up(i).wait_send()
            low_down(i).wait_send()
            outer_up(i).wait_send()
            outer_down(i).wait_send()

        chord_up(i).wait_send()
        chord_down(i).wait_send()
        for d in range(1, GROUP):
            group_send(i, d).wait_send()
        for d in range(1, groups):
            total_send(i, d).wait_send()

        @pl.when(inner)
        def _():
            for h in range(2):
                a_copy(i, h).wait_send()
                x_copy(i, h).wait_send()

        @pl.when(outer_dev)
        def _():
            for h in range(2):
                y_copy(i, h).wait_send()

        return c

    lax.fori_loop(0, Q, drain, 0)
    for d in range(1, SPANS):
        load_span(d).wait_send()

    def load_end(d, acc):
        load_wrap(d).wait()
        return acc + lrb[d - 1]

    final = lax.fori_loop(1, WRAPS, load_end, ld[wrap])
    for k in range(3):
        loads[k] = final[k : k + 1, 0:each]


def local(state, state_old, wrap_rate, span_rate, blank, section):
    def vm(*shape):
        return pltpu.VMEM(shape, jnp.float32)

    def im(*shape):
        return pltpu.VMEM(shape, jnp.int32)

    dma = pltpu.SemaphoreType.DMA
    scratch = [
        vm(Q, S, W, N), vm(Q, S, W, N), vm(Q, S, N), vm(Q, W, N), im(S, W, N // 2), im(S, H, N), im(S, W),
        vm(Q, S, H, N), vm(Q, S, H, N), vm(Q, S, H, N), vm(Q, S, H, N), vm(Q, S, H, N), vm(Q, S, W + 16, N),
        vm(Q, 2, W, N), vm(Q, 2, W, N), vm(Q, 2, H, N), vm(Q, 2, H, N), vm(Q, 2, H, N), vm(Q, 2, H, N),
        vm(Q, 8, N), vm(Q, 8, N), vm(Q, 8, N), vm(Q, 8, N), vm(Q, S, W, N),
        vm(Q, S, W + 8, N), vm(Q, S, W + 8, N), vm(Q, S, W + 8, N), vm(Q, S, W + 8, N), vm(Q, S, 16, N),
        vm(8, N), vm(Q, 8, 8, N), vm(Q, 2, 8, N), vm(Q, GROUP, 2, 8, N), vm(Q, 2, 8, N), vm(Q, WRAPS // GROUP, 2, 8, N),
        vm(2, 8, N), vm(Q, S, W, N), vm(Q, 9, W, N), vm(Q, 10, W, N), vm(Q, 8, W, N), vm(Q, W, N), vm(Q, W, N),
        vm(Q, 2, 2, H, N), vm(Q, 2, 2, H, N), vm(Q, 2, 2, H, N), vm(Q, 2, 2, H, N), vm(Q, 2, 2, H, N), vm(Q, 2, 2, H, N),
        vm(S, W, N), vm(SPANS, 8, 256), vm(SPANS - 1, 8, 256), vm(WRAPS, 8, N), vm(WRAPS - 1, 8, N),
        dma((5,)), dma((V,)), dma((2, Q)), dma((2, Q)), dma((2,)), dma((2,)), dma((2, Q)), dma((2, Q)),
        dma((2, Q)), dma((2, Q)), dma((2, Q)), dma((2, Q)),
        dma((Q, GROUP - 1)), dma((Q, GROUP - 1)), dma((Q, WRAPS // GROUP - 1)), dma((Q, WRAPS // GROUP - 1)),
        dma((Q, 2)), dma((Q, 2)), dma((Q, 2)), dma((Q, 2)), dma((Q, 2)), dma((Q, 2)),
        dma((SPANS - 1,)), dma((SPANS - 1,)), dma((WRAPS - 1,)), dma((WRAPS - 1,)),
    ]
    each = SECTIONS // (SPANS * WRAPS)
    updated, loads = pl.pallas_call(
        kernel,
        out_shape=(
            jax.ShapeDtypeStruct(state.shape, jnp.float32),
            jax.ShapeDtypeStruct((3, 1, each), jnp.float32),
        ),
        in_specs=[pl.BlockSpec(memory_space=pltpu.HBM)] * 6,
        out_specs=(pl.BlockSpec(memory_space=pltpu.VMEM), pl.BlockSpec(memory_space=pltpu.VMEM)),
        scratch_shapes=scratch,
        compiler_params=pltpu.CompilerParams(
            collective_id=0, has_side_effects=True, vmem_limit_bytes=50_000_000),
    )(*[pltpu.with_memory_space_constraint(a, pltpu.HBM) for a in (state, state_old, wrap_rate, span_rate, blank, section)])
    return updated, jnp.transpose(loads, (1, 0, 2))


def solution(mesh):
    return jax.shard_map(
        local,
        mesh=mesh,
        in_specs=(
            P("blade", None, "span", "wrap", None),
            P("blade", None, "span", "wrap", None),
            P("blade", None, "span", None),
            P("blade", None, "wrap", None),
            P("blade", "span", "wrap", None),
            P("blade", "span", "wrap"),
        ),
        out_specs=(P("blade", None, "span", "wrap", None), P("blade", None, ("span", "wrap"))),
        check_vma=False,
    )
```

```python
import jax
import jax.numpy as jnp
from jax import lax
from jax.experimental import pallas as pl
from jax.experimental.pallas import tpu as pltpu
from jax.sharding import PartitionSpec as P

MESH = pl.DeviceIdType.MESH
SECTIONS = 640
V, S, W, N = 5, 4, 64, 128
Q = V + 1
H = W // 2
GROUP = 8
SPANS, WRAPS, BLADES = 4, 16, 4
LEVELS = 6


def line_roots(r):
    ri = 1.0 / r
    y = 6.0 + ri + jnp.sqrt(ri * (12.0 + ri))
    q = 2.0 / ((y - 2.0) + jnp.sqrt(y * (y - 4.0)))
    p = 6.0 * q / (1.0 + q)
    return p, q


def square(m):
    a, b, c, d = m
    bc = b * c
    tr = a + d
    return a * a + bc, b * tr, c * tr, d * d + bc


RESIDUAL, TOTAL, CARRY, INNER_AHEAD, INNER_BACK, OUTER_BACK = 3, 6, 8, 10, 12, 14
WALL_TICKS = (1, 3, 5, 7, 9, 11)
LOAD_PART, LOAD_SUM = 12, 14


def kernel(
    state, old, wrate, srate, blank, section,
    out, loads,
    st, so, wr, sr, bl, mk, sec, pk, lk, op, fb, fa, fl, hlo, hhi, llo, lhi, olo, ohi, cslo, cshi, crlo, crhi, fr,
    ga, gd, ub, ud, cf, r8, tm, ms, m1, gs, m2, cc, xb, l1t, l2t, rdt, alt, bet,
    ysend, yrecv, asend, arecv, xsend, xrecv, ob, la, lra, ld, lrb,
    in_s, st_s, fs, fq, hs, hq, ls, lq, os_, oq, cs, cq, r1s, r1q, r2s, r2q, ys, yq, as_, aq, xs, xq,
    las, laq, lbs, lbq,
):
    span = lax.axis_index("span")
    wrap = lax.axis_index("wrap")
    blade = lax.axis_index("blade")
    place = wrap % GROUP
    group = wrap // GROUP
    groups = WRAPS // GROUP

    barrier = pltpu.get_barrier_semaphore()
    for d in range(1, WRAPS):
        pl.semaphore_signal(barrier, inc=1, device_id={"wrap": (wrap + d) % WRAPS}, device_id_type=MESH)
    for d in range(1, SPANS):
        pl.semaphore_signal(barrier, inc=1, device_id={"span": (span + d) % SPANS}, device_id_type=MESH)
    for d in (1, BLADES - 1):
        pl.semaphore_signal(barrier, inc=1, device_id={"blade": (blade + d) % BLADES}, device_id_type=MESH)

    copy_wr = pltpu.make_async_copy(wrate.at[0], wr.at[1:Q], in_s.at[0])
    copy_st = [pltpu.make_async_copy(state.at[0, v], st.at[v + 1], st_s.at[v]) for v in range(V)]
    copy_bl = pltpu.make_async_copy(blank.at[0], bl, in_s.at[1])
    copy_sr = pltpu.make_async_copy(srate.at[0], sr.at[1:Q], in_s.at[2])
    copy_so = pltpu.make_async_copy(old.at[0], so.at[1:Q], in_s.at[3])
    copy_sec = pltpu.make_async_copy(section.at[0], sec, in_s.at[4])
    for copy in [copy_wr] + copy_st + [copy_bl, copy_sr, copy_so, copy_sec]:
        copy.start()

    lane_h = lax.broadcasted_iota(jnp.int32, (H, N), 1)
    lane_w = lax.broadcasted_iota(jnp.int32, (W, N), 1)
    row_w = lax.broadcasted_iota(jnp.int32, (W, N), 0)
    row_8 = lax.broadcasted_iota(jnp.int32, (8, N), 0)

    def wall_lanes(a, b, c, rest):
        lane = lax.broadcasted_iota(jnp.int32, a.shape, 1)
        return jnp.where(
            lane < 4, a, jnp.where(lane < 8, pltpu.roll(b, 4, 1), jnp.where(lane < 12, pltpu.roll(c, 8, 1), rest)))

    copy_wr.wait()
    wr[0] = wall_lanes(wr[2], wr[3], wr[4], 1.0)

    def chord_tables(idx, c):
        i = idx // S
        s = idx % S
        r = jnp.broadcast_to(wr[i, pl.ds(s, 1), :], (8, N))
        p, q = line_roots(r)
        g0 = (1.0 + q) * (2.0 * q) / (r * (1.0 - q) * (1.0 + q - p) * (1.0 + q + p))
        ratio = p / (1.0 + q)
        g1 = g0 * ratio
        pk_, qk_ = [p], [q]
        for k in range(LEVELS - 1):
            pk_.append(pk_[-1] * pk_[-1] - 2.0 * qk_[-1])
            qk_.append(qk_[-1] * qk_[-1])
        rows = pk_ + qk_ + [g0, -g1 * q, g1, -q * g0]

        def pick(values):
            tile = values[0]
            for n in range(1, 8):
                tile = jnp.where(row_8 == n, values[n], tile)
            return tile

        cf[i, s, 0:8, :] = pick(rows[0:8])
        cf[i, s, 8:16, :] = pick(rows[8:16])
        g = [g0, g1]
        for n in range(2, 17):
            g.append(p * g[-1] - q * g[-2])
        zero = jnp.zeros_like(p)
        u = [zero, zero + 1.0]
        for n in range(2, 17):
            u.append(p * u[-1] - q * u[-2])
        p3, q3 = pk_[3], qk_[3]

        def ascend(table, first, second):
            table[i, s, 0:8, :] = first
            table[i, s, 8:16, :] = second
            before, now = first, second
            for t in range(2, 9):
                before, now = now, p3 * now - q3 * before
                table[i, s, 8 * t : 8 * t + 8, :] = now

        def descend(table, last, first, second):
            table[i, s, 64:72, :] = last
            table[i, s, 56:64, :] = first
            table[i, s, 48:56, :] = second
            before, now = first, second
            for t in range(5, -1, -1):
                before, now = now, p3 * now - q3 * before
                table[i, s, 8 * t : 8 * t + 8, :] = now

        ascend(ga, pick(g[0:8]), pick(g[8:16]))
        descend(gd, jnp.where(row_8 == 0, g0, 0.0), pick(g[8:0:-1]), pick(g[16:8:-1]))
        ascend(ub, pick(u[0:8]), pick(u[8:16]))
        descend(ud, zero, pick(u[8:0:-1]), pick(u[16:8:-1]))
        return c

    lax.fori_loop(0, Q * S, chord_tables, 0)

    for copy in copy_st:
        copy.wait()

    def pack(i, c):
        for s in range(S):
            low = st[i, s, 0:H, :]
            high = st[i, s, H:W, :]
            pk[i, s] = jnp.where(lane_h < N // 2, pltpu.roll(low, N // 2, 1), high)
            lk[i, s] = jnp.where(lane_h < N // 2, low, pltpu.roll(high, N // 2, 1))
        return c

    lax.fori_loop(1, Q, pack, 0)

    for s in range(S):
        wall = wall_lanes(st[2, s], st[3, s], st[4, s], 0.0)
        fl[0, s, 8 : 8 + W, :] = wall
        cslo[0, 2 * s : 2 * s + 2, :] = wall[0:2]
        cshi[0, 2 * s : 2 * s + 2, :] = wall[W - 2 : W]

    def fringe_up(i):
        return pltpu.make_async_remote_copy(
            src_ref=pk.at[i], dst_ref=fb.at[i], send_sem=fs.at[0, i], recv_sem=fq.at[0, i],
            device_id={"blade": (blade + 1) % BLADES}, device_id_type=MESH)

    def fringe_down(i):
        return pltpu.make_async_remote_copy(
            src_ref=pk.at[i], dst_ref=fa.at[i], send_sem=fs.at[1, i], recv_sem=fq.at[1, i],
            device_id={"blade": (blade + BLADES - 1) % BLADES}, device_id_type=MESH)

    above = (span + 1) % SPANS
    below = (span + SPANS - 1) % SPANS

    def wall_up():
        return pltpu.make_async_remote_copy(
            src_ref=fl.at[0, 2:4, 8 : 8 + W, :], dst_ref=hlo.at[0], send_sem=hs.at[0], recv_sem=hq.at[0],
            device_id={"span": above}, device_id_type=MESH)

    def wall_down():
        return pltpu.make_async_remote_copy(
            src_ref=fl.at[0, 0:2, 8 : 8 + W, :], dst_ref=hhi.at[0], send_sem=hs.at[1], recv_sem=hq.at[1],
            device_id={"span": below}, device_id_type=MESH)

    def low_up(i):
        return pltpu.make_async_remote_copy(
            src_ref=lk.at[i, 2:4], dst_ref=llo.at[i], send_sem=ls.at[0, i], recv_sem=lq.at[0, i],
            device_id={"span": above}, device_id_type=MESH)

    def low_down(i):
        return pltpu.make_async_remote_copy(
            src_ref=lk.at[i, 0:2], dst_ref=lhi.at[i], send_sem=ls.at[1, i], recv_sem=lq.at[1, i],
            device_id={"span": below}, device_id_type=MESH)

    def outer_up(i):
        return pltpu.make_async_remote_copy(
            src_ref=op.at[i, 2:4], dst_ref=olo.at[i], send_sem=os_.at[0, i], recv_sem=oq.at[0, i],
            device_id={"span": above}, device_id_type=MESH)

    def outer_down(i):
        return pltpu.make_async_remote_copy(
            src_ref=op.at[i, 0:2], dst_ref=ohi.at[i], send_sem=os_.at[1, i], recv_sem=oq.at[1, i],
            device_id={"span": below}, device_id_type=MESH)

    def chord_up(i):
        return pltpu.make_async_remote_copy(
            src_ref=cshi.at[i], dst_ref=crlo.at[i], send_sem=cs.at[0, i], recv_sem=cq.at[0, i],
            device_id={"wrap": (wrap + 1) % WRAPS}, device_id_type=MESH)

    def chord_down(i):
        return pltpu.make_async_remote_copy(
            src_ref=cslo.at[i], dst_ref=crhi.at[i], send_sem=cs.at[1, i], recv_sem=cq.at[1, i],
            device_id={"wrap": (wrap + WRAPS - 1) % WRAPS}, device_id_type=MESH)

    def group_send(i, d):
        target = group * GROUP + (place + d) % GROUP
        return pltpu.make_async_remote_copy(
            src_ref=ms.at[i], dst_ref=m1.at[i, place], send_sem=r1s.at[i, d - 1], recv_sem=r1q.at[i, d - 1],
            device_id={"wrap": target}, device_id_type=MESH)

    def total_send(i, d):
        target = (group + d) % groups * GROUP + place
        return pltpu.make_async_remote_copy(
            src_ref=gs.at[i], dst_ref=m2.at[i, group], send_sem=r2s.at[i, d - 1], recv_sem=r2q.at[i, d - 1],
            device_id={"wrap": target}, device_id_type=MESH)

    pl.semaphore_wait(barrier, 2 + SPANS - 1 + WRAPS - 1)

    def first_sends(i, c):
        fringe_up(i).start()
        fringe_down(i).start()
        return c

    def low_sends(i, c):
        low_up(i).start()
        low_down(i).start()
        return c

    lax.fori_loop(1, Q, first_sends, 0)
    wall_up().start()
    wall_down().start()
    chord_up(0).start()
    chord_down(0).start()
    lax.fori_loop(1, Q, low_sends, 0)

    for copy in (copy_bl, copy_sr, copy_so, copy_sec):
        copy.wait()

    for s in range(S):
        mk[s] = jnp.concatenate([bl[s, 0:H, :], bl[s, H:W, :]], axis=-1)
        so[0, s] = wall_lanes(so[2, s], so[3, s], so[4, s], 0.0)
    sr[0] = wall_lanes(sr[2], sr[3], sr[4], 1.0)

    def transfers(i, c):
        rate = wr[i]
        r8[0:S, :] = rate
        r8[S : 2 * S, :] = rate
        p, q = line_roots(r8[...])
        m = (p, -q, jnp.ones_like(p), jnp.zeros_like(p))
        for k in range(LEVELS):
            m = square(m)
        for k in range(4):
            tm[i, k] = m[k]
        m = square(square(square(m)))
        for k in range(4):
            tm[i, 4 + k] = m[k]
        return c

    lax.fori_loop(0, Q, transfers, 0)

    def span_tables(idx, c):
        i = idx // 8
        rows = pl.ds(pl.multiple_of((idx % 8) * 8, 8), 8)
        r = sr[i, rows, :]
        centre = 1.0 + 5.0 * r
        first = -3.0 * r
        second = 0.5 * r
        zero = jnp.zeros_like(r)
        one_l, two_l, rd = [zero], [zero], [1.0 / centre]
        for j in range(1, 10):
            two = second * rd[j - 2] if j >= 2 else zero
            two_l.append(two)
            if j == 9:
                break
            top = first - second * one_l[j - 1]
            one = top * rd[j - 1]
            one_l.append(one)
            if j < 8:
                rd.append(1.0 / (centre - one * top - two * second))
        for j in range(9):
            l1t[i, j, rows, :] = one_l[j]
        for j in range(10):
            l2t[i, j, rows, :] = two_l[j]
        for j in range(8):
            rdt[i, j, rows, :] = rd[j]
        alpha = 1.0 - two_l[9] * two_l[8]
        beta = one_l[8] - two_l[9] * one_l[7]
        det = 1.0 / ((alpha - beta) * (alpha + beta))
        alt[i, rows, :] = alpha * det
        bet[i, rows, :] = beta * det
        return c

    lax.fori_loop(0, Q * 8, span_tables, 0)

    def fields(i):
        fringe_up(i).wait_recv()
        fringe_down(i).wait_recv()
        for s in range(S):
            marks = mk[s]
            op[i, s] = jnp.where(marks == 1, fb[i, s], jnp.where(marks == 2, fa[i, s], pk[i, s]))
        outer_up(i).start()
        outer_down(i).start()
        for s in range(S):
            outer = op[i, s]
            low = jnp.where(lane_h >= N // 2, pltpu.roll(outer, N // 2, 1), st[i, s, 0:H, :])
            high = jnp.where(lane_h >= N // 2, outer, st[i, s, H:W, :])
            fl[i, s, 8 : 8 + H, :] = low
            fl[i, s, 8 + H : 8 + W, :] = high
            cslo[i, 2 * s : 2 * s + 2, :] = low[0:2]
            cshi[i, 2 * s : 2 * s + 2, :] = high[H - 2 : H]
        chord_up(i).start()
        chord_down(i).start()

    has_low = jnp.where(span > 0, 1.0, 0.0)
    has_high = jnp.where(span < SPANS - 1, 1.0, 0.0)

    def residuals(i):
        chord_up(i).wait_recv()
        chord_down(i).wait_recv()

        @pl.when(i == 0)
        def _():
            wall_up().wait_recv()
            wall_down().wait_recv()

        @pl.when(i > 0)
        def _():
            low_up(i).wait_recv()
            low_down(i).wait_recv()
            outer_up(i).wait_recv()
            outer_down(i).wait_recv()
            for low, outer, whole in ((llo, olo, hlo), (lhi, ohi, hhi)):
                for k in range(2):
                    whole[i, k, 0:H, :] = jnp.where(lane_h < N // 2, low[i, k], pltpu.roll(outer[i, k], N // 2, 1))
                    whole[i, k, H:W, :] = jnp.where(lane_h < N // 2, pltpu.roll(low[i, k], N // 2, 1), outer[i, k])

        for s in range(S):
            fl[i, s, 6:8, :] = crlo[i, 2 * s : 2 * s + 2, :]
            fl[i, s, 8 + W : 10 + W, :] = crhi[i, 2 * s : 2 * s + 2, :]

        def station(t):
            if t < 0:
                return hlo[i, t + 2] * has_low
            if t >= S:
                return hhi[i, t - S] * has_high
            return fl[i, t, 8 : 8 + W, :]

        inside = (lane_w & jnp.where(i == 0, 3, N - 1)) > 0
        for s in range(S):
            own = fl[i, s, 8 : 8 + W, :]
            ahead = jnp.where(lane_w < N - 1, pltpu.roll(own, N - 1, 1), 0.0)
            behind = jnp.where(inside, pltpu.roll(own, 1, 1), 0.0)
            wide = fl[i, s, 10 : 10 + W, :] + fl[i, s, 6 : 6 + W, :] + station(s + 2) + station(s - 2)
            plus = fl[i, s, 9 : 9 + W, :] + station(s + 1)
            minus = fl[i, s, 7 : 7 + W, :] + station(s - 1)
            rhs = (so[i, s] - 2.1 * own) + 0.25 * (ahead + behind) - 0.05 * wide - 0.3 * plus + 0.7 * minus
            fr[i, s] = rhs
            ms[i, 0, s : s + 1, :] = jnp.sum(gd[i, s, 0:W, :] * rhs, axis=0, keepdims=True)
            ms[i, 1, s : s + 1, :] = jnp.sum(gd[i, s, 1 : 1 + W, :] * rhs, axis=0, keepdims=True)
            ms[i, 0, S + s : S + s + 1, :] = jnp.sum(ga[i, s, 1 : 1 + W, :] * rhs, axis=0, keepdims=True)
            ms[i, 1, S + s : S + s + 1, :] = jnp.sum(ga[i, s, 0:W, :] * rhs, axis=0, keepdims=True)
        m1[i, place] = ms[i]
        for d in (4, 3, 5, 2, 6, 1, 7):
            group_send(i, d).start()

    def down(x, n):
        if n % 8 == 0:
            return jnp.concatenate([jnp.zeros((n, N), jnp.float32), x[: W - n]], axis=0)
        return jnp.where(row_w >= n, pltpu.roll(x, n, 0), 0.0)

    def up(x, n):
        if n % 8 == 0:
            return jnp.concatenate([x[n:], jnp.zeros((n, N), jnp.float32)], axis=0)
        return jnp.where(row_w < W - n, pltpu.roll(x, W - n, 0), 0.0)

    def sweeps(i, s):
        rhs = fr[i, s]

        def coef(k):
            return cf[i, s, k : k + 1, :]

        ahead = coef(12) * rhs + coef(13) * down(rhs, 1)
        back = coef(14) * up(rhs, 1) + coef(15) * up(rhs, 2)
        for k in range(LEVELS):
            n = 1 << k
            pc, qc = coef(k), coef(LEVELS + k)
            if 2 * n < W:
                ahead = ahead + pc * down(ahead, n) + qc * down(ahead, 2 * n)
                back = back + pc * up(back, n) + qc * up(back, 2 * n)
            else:
                ahead = ahead + pc * down(ahead, n)
                back = back + pc * up(back, n)
        xb[i, s] = ahead + back

    forward = row_8 < S
    steps = jnp.where(forward, place, GROUP - 1 - place)
    zero_8 = jnp.zeros((8, N), jnp.float32)

    def advance(t, acc, x):
        return (t[0] * acc[0] + t[1] * acc[1] + x[0], t[2] * acc[0] + t[3] * acc[1] + x[1])

    def ordered(ref, i, a, b):
        return tuple(jnp.where(forward, ref[i, a, k], ref[i, b, k]) for k in range(2))

    def totals(i):
        for d in range(1, GROUP):
            group_send(i, d).wait_recv()
        t = [tm[i, k] for k in range(4)]
        acc = (zero_8, zero_8)
        for j in range(GROUP):
            acc = advance(t, acc, ordered(m1, i, j, GROUP - 1 - j))
        gs[i, 0] = acc[0]
        gs[i, 1] = acc[1]
        for d in range(1, groups):
            total_send(i, d).start()
        m2[i, group, 0] = acc[0]
        m2[i, group, 1] = acc[1]

    low_side = span < SPANS // 2
    inner = (span == 1) | (span == 2)
    outer_dev = (span == 0) | (span == SPANS - 1)
    mate = jnp.where(span % 2 == 0, span + 1, span - 1)

    def half(h):
        return pl.ds(pl.multiple_of(h * H, 8), H)

    def spot(j):
        return jnp.where(low_side, j, S - 1 - j)

    def y_copy(i, h):
        return pltpu.make_async_remote_copy(
            src_ref=ysend.at[i, h], dst_ref=yrecv.at[i, h], send_sem=ys.at[i, h], recv_sem=yq.at[i, h],
            device_id={"span": mate}, device_id_type=MESH)

    def a_copy(i, h):
        return pltpu.make_async_remote_copy(
            src_ref=asend.at[i, h], dst_ref=arecv.at[i, h], send_sem=as_.at[i, h], recv_sem=aq.at[i, h],
            device_id={"span": SPANS - 1 - span}, device_id_type=MESH)

    def x_copy(i, h):
        return pltpu.make_async_remote_copy(
            src_ref=xsend.at[i, h], dst_ref=xrecv.at[i, h], send_sem=xs.at[i, h], recv_sem=xq.at[i, h],
            device_id={"span": mate}, device_id_type=MESH)

    def carried(i):
        for d in range(1, groups):
            total_send(i, d).wait_recv()
        t = [tm[i, k] for k in range(4)]
        t4 = [tm[i, 4 + k] for k in range(4)]
        acc = (zero_8, zero_8)
        for turn in range(2):
            for d in range(groups, 0, -1):
                acc = advance(t4, acc, ordered(m2, i, (group + groups - d) % groups, (group + d) % groups))
        for j in range(GROUP - 1):
            nxt = advance(t, acc, ordered(m1, i, j, GROUP - 1 - j))
            acc = tuple(jnp.where(j < steps, b, a) for a, b in zip(acc, nxt))
        cc[0] = acc[0]
        cc[1] = acc[1]
        for s in range(S):
            minus_q = -cf[i, s, LEVELS : LEVELS + 1, :]
            xb[i, s] = (
                xb[i, s]
                + ub[i, s, 1 : 1 + W, :] * cc[0, s : s + 1, :]
                + ub[i, s, 0:W, :] * (minus_q * cc[1, s : s + 1, :])
                + ud[i, s, 0:W, :] * cc[0, S + s : S + s + 1, :]
                + ud[i, s, 1 : 1 + W, :] * (minus_q * cc[1, S + s : S + s + 1, :])
            )

        @pl.when(outer_dev)
        def _():
            def part(h, c):
                rows = half(h)
                y = []
                for j in range(S):
                    now = xb[i, spot(j), rows, :]
                    if j >= 1:
                        now = now - l1t[i, j, rows, :] * y[j - 1]
                    if j >= 2:
                        now = now - l2t[i, j, rows, :] * y[j - 2]
                    y.append(now)
                    xb[i, spot(j), rows, :] = now * rdt[i, j, rows, :]
                ysend[i, h, 0] = y[S - 2]
                ysend[i, h, 1] = y[S - 1]
                y_copy(i, h).start()
                return c

            lax.fori_loop(0, 2, part, 0)

    def inner_forward(i):
        def part(h, c):
            rows = half(h)
            y_copy(i, h).wait_recv()
            y = [yrecv[i, h, 0], yrecv[i, h, 1]]
            for j in range(S):
                now = xb[i, spot(j), rows, :] - l1t[i, S + j, rows, :] * y[-1] - l2t[i, S + j, rows, :] * y[-2]
                y.append(now)
                scaled = now * rdt[i, S + j, rows, :]
                xb[i, spot(j), rows, :] = scaled
                if j >= S - 2:
                    asend[i, h, j - (S - 2)] = scaled
            a_copy(i, h).start()
            return c

        lax.fori_loop(0, 2, part, 0)

    def finish(i, h, xs_):
        rows = half(h)
        own = pl.ds(pl.multiple_of(8 + h * H, 8), H)
        spots_ = [spot(j) for j in range(S)]
        done = [fl[i, at, own, :] + x for at, x in zip(spots_, xs_)]

        @pl.when(i > 0)
        def _():
            for at, value in zip(spots_, done):
                out[0, i - 1, at, rows, :] = value

        @pl.when(i == 0)
        def _():
            for at, value in zip(spots_, done):
                ob[at, rows, :] = value

    def inner_back(i):
        def part(h, c):
            rows = half(h)

            def one(j):
                return l1t[i, j, rows, :]

            def two(j):
                return l2t[i, j, rows, :]

            a_copy(i, h).wait_recv()
            a6, a7 = xb[i, spot(2), rows, :], xb[i, spot(3), rows, :]
            b6, b7 = arecv[i, h, 0], arecv[i, h, 1]
            lead = a7 - two(9) * b6
            other = b7 - two(9) * a6
            x7 = alt[i, rows, :] * lead - bet[i, rows, :] * other
            x8 = alt[i, rows, :] * other - bet[i, rows, :] * lead
            x6 = a6 - one(7) * x7 - two(8) * x8
            x5 = xb[i, spot(1), rows, :] - one(6) * x6 - two(7) * x7
            x4 = xb[i, spot(0), rows, :] - one(5) * x5 - two(6) * x6
            xsend[i, h, 0] = x4
            xsend[i, h, 1] = x5
            x_copy(i, h).start()
            finish(i, h, (x4, x5, x6, x7))
            return c

        lax.fori_loop(0, 2, part, 0)

    def outer_back(i):
        def part(h, c):
            rows = half(h)
            x_copy(i, h).wait_recv()
            x = [xrecv[i, h, 1], xrecv[i, h, 0]]
            for j in range(S - 1, -1, -1):
                x.append(xb[i, spot(j), rows, :] - l1t[i, j + 1, rows, :] * x[-1] - l2t[i, j + 2, rows, :] * x[-2])
            finish(i, h, x[:1:-1])
            return c

        lax.fori_loop(0, 2, part, 0)

    part = SECTIONS // SPANS
    padded = 256
    each = part // WRAPS

    def load_span(d):
        return pltpu.make_async_remote_copy(
            src_ref=la.at[(span + d) % SPANS], dst_ref=lra.at[d - 1], send_sem=las.at[d - 1], recv_sem=laq.at[d - 1],
            device_id={"span": (span + d) % SPANS}, device_id_type=MESH)

    def load_wrap(d):
        target = (wrap + d) % WRAPS
        return pltpu.make_async_remote_copy(
            src_ref=ld.at[target], dst_ref=lrb.at[d - 1], send_sem=lbs.at[d - 1], recv_sem=lbq.at[d - 1],
            device_id={"wrap": target}, device_id_type=MESH)

    def load_parts():
        walls, names = [], []
        for s in range(S):
            value = ob[s]
            step = pltpu.roll(value, N - 1, 1) - value
            wall = jnp.where(
                lane_w == 0, step, jnp.where(
                    lane_w == 1, pltpu.roll(step, N - 3, 1), jnp.where(
                        lane_w == 2, pltpu.roll(step, N - 6, 1), 0.0)))
            walls.append(jnp.transpose(wall)[0:8, :])
            name = sec[s : s + 1, :]
            for k in range(1, SPANS):
                name = name + jnp.where(sec[s : s + 1, :] >= k * part, padded - part, 0)
            names.append(name)
        nodes = jnp.concatenate(walls, axis=1)
        spots = lax.broadcasted_iota(jnp.int32, (SPANS * padded, S * W), 0)
        picks = jnp.where(spots == jnp.concatenate(names, axis=1), 1.0, 0.0).astype(jnp.bfloat16)
        parts = []
        for k in range(3):
            piece = nodes.astype(jnp.bfloat16)
            nodes = nodes - piece.astype(jnp.float32)
            parts.append(piece.astype(jnp.float32))
        stacked = jnp.concatenate(parts + [jnp.zeros_like(nodes)], axis=0).astype(jnp.bfloat16)
        sums = lax.dot_general(
            stacked, picks, (((1,), (1,)), ((), ())), preferred_element_type=jnp.float32)
        total = sums[0:8] + sums[8:16] + sums[16:24]
        for k in range(SPANS):
            la[k] = total[:, k * padded : (k + 1) * padded]
        for d in range(1, SPANS):
            load_span(d).start()

    def load_sums():
        for d in range(1, SPANS):
            load_span(d).wait_recv()
        mine = la[span]
        for d in range(1, SPANS):
            mine = mine + lra[d - 1]
        for k in range(WRAPS):
            ld[k] = (mine if k == 0 else pltpu.roll(mine, padded - each * k, 1))[:, 0:N]

        def load_start(d, c):
            load_wrap(d).start()
            return c

        lax.fori_loop(1, WRAPS, load_start, 0)

    def tick(t, c):
        def stage(offset, wall, body, role=True):
            i = jnp.where(t == wall, 0, t - offset)

            @pl.when(((t == wall) | ((i >= 1) & (i < Q))) & role)
            def _():
                body(i)

        def chord_stage(i):
            residuals(i)

            def one(s, c):
                sweeps(i, s)
                return c

            lax.fori_loop(0, S, one, 0)

        @pl.when(t < Q)
        def _():
            fields(t)

        stage(RESIDUAL, WALL_TICKS[0], chord_stage)
        stage(TOTAL, WALL_TICKS[1], totals)
        stage(CARRY, WALL_TICKS[2], carried)
        stage(INNER_AHEAD, WALL_TICKS[3], inner_forward, inner)
        stage(INNER_BACK, WALL_TICKS[4], inner_back, inner)
        stage(OUTER_BACK, WALL_TICKS[5], outer_back, outer_dev)

        @pl.when(t == LOAD_PART)
        def _():
            load_parts()

        @pl.when(t == LOAD_SUM)
        def _():
            load_sums()

        return c

    lax.fori_loop(1, Q + OUTER_BACK, tick, 0)

    for copy in (wall_up(), wall_down()):
        copy.wait_send()

    def drain(i, c):
        @pl.when(i > 0)
        def _():
            fringe_up(i).wait_send()
            fringe_down(i).wait_send()
            low_up(i).wait_send()
            low_down(i).wait_send()
            outer_up(i).wait_send()
            outer_down(i).wait_send()

        chord_up(i).wait_send()
        chord_down(i).wait_send()
        for d in range(1, GROUP):
            group_send(i, d).wait_send()
        for d in range(1, groups):
            total_send(i, d).wait_send()

        @pl.when(inner)
        def _():
            for h in range(2):
                a_copy(i, h).wait_send()
                x_copy(i, h).wait_send()

        @pl.when(outer_dev)
        def _():
            for h in range(2):
                y_copy(i, h).wait_send()

        return c

    lax.fori_loop(0, Q, drain, 0)
    for d in range(1, SPANS):
        load_span(d).wait_send()

    def load_end(d, acc):
        load_wrap(d).wait()
        return acc + lrb[d - 1]

    final = lax.fori_loop(1, WRAPS, load_end, ld[wrap])
    for k in range(3):
        loads[k] = final[k : k + 1, 0:each]


def local(state, state_old, wrap_rate, span_rate, blank, section):
    def vm(*shape):
        return pltpu.VMEM(shape, jnp.float32)

    def im(*shape):
        return pltpu.VMEM(shape, jnp.int32)

    dma = pltpu.SemaphoreType.DMA
    scratch = [
        vm(Q, S, W, N), vm(Q, S, W, N), vm(Q, S, N), vm(Q, W, N), im(S, W, N // 2), im(S, H, N), im(S, W),
        vm(Q, S, H, N), vm(Q, S, H, N), vm(Q, S, H, N), vm(Q, S, H, N), vm(Q, S, H, N), vm(Q, S, W + 16, N),
        vm(Q, 2, W, N), vm(Q, 2, W, N), vm(Q, 2, H, N), vm(Q, 2, H, N), vm(Q, 2, H, N), vm(Q, 2, H, N),
        vm(Q, 8, N), vm(Q, 8, N), vm(Q, 8, N), vm(Q, 8, N), vm(Q, S, W, N),
        vm(Q, S, W + 8, N), vm(Q, S, W + 8, N), vm(Q, S, W + 8, N), vm(Q, S, W + 8, N), vm(Q, S, 16, N),
        vm(8, N), vm(Q, 8, 8, N), vm(Q, 2, 8, N), vm(Q, GROUP, 2, 8, N), vm(Q, 2, 8, N), vm(Q, WRAPS // GROUP, 2, 8, N),
        vm(2, 8, N), vm(Q, S, W, N), vm(Q, 9, W, N), vm(Q, 10, W, N), vm(Q, 8, W, N), vm(Q, W, N), vm(Q, W, N),
        vm(Q, 2, 2, H, N), vm(Q, 2, 2, H, N), vm(Q, 2, 2, H, N), vm(Q, 2, 2, H, N), vm(Q, 2, 2, H, N), vm(Q, 2, 2, H, N),
        vm(S, W, N), vm(SPANS, 8, 256), vm(SPANS - 1, 8, 256), vm(WRAPS, 8, N), vm(WRAPS - 1, 8, N),
        dma((5,)), dma((V,)), dma((2, Q)), dma((2, Q)), dma((2,)), dma((2,)), dma((2, Q)), dma((2, Q)),
        dma((2, Q)), dma((2, Q)), dma((2, Q)), dma((2, Q)),
        dma((Q, GROUP - 1)), dma((Q, GROUP - 1)), dma((Q, WRAPS // GROUP - 1)), dma((Q, WRAPS // GROUP - 1)),
        dma((Q, 2)), dma((Q, 2)), dma((Q, 2)), dma((Q, 2)), dma((Q, 2)), dma((Q, 2)),
        dma((SPANS - 1,)), dma((SPANS - 1,)), dma((WRAPS - 1,)), dma((WRAPS - 1,)),
    ]
    each = SECTIONS // (SPANS * WRAPS)
    updated, loads = pl.pallas_call(
        kernel,
        out_shape=(
            jax.ShapeDtypeStruct(state.shape, jnp.float32),
            jax.ShapeDtypeStruct((3, 1, each), jnp.float32),
        ),
        in_specs=[pl.BlockSpec(memory_space=pltpu.HBM)] * 6,
        out_specs=(pl.BlockSpec(memory_space=pltpu.VMEM), pl.BlockSpec(memory_space=pltpu.VMEM)),
        scratch_shapes=scratch,
        compiler_params=pltpu.CompilerParams(
            collective_id=0, has_side_effects=True, vmem_limit_bytes=50_000_000),
    )(*[pltpu.with_memory_space_constraint(a, pltpu.HBM) for a in (state, state_old, wrap_rate, span_rate, blank, section)])
    return updated, jnp.transpose(loads, (1, 0, 2))


def solution(mesh):
    return jax.shard_map(
        local,
        mesh=mesh,
        in_specs=(
            P("blade", None, "span", "wrap", None),
            P("blade", None, "span", "wrap", None),
            P("blade", None, "span", None),
            P("blade", None, "wrap", None),
            P("blade", "span", "wrap", None),
            P("blade", "span", "wrap"),
        ),
        out_specs=(P("blade", None, "span", "wrap", None), P("blade", None, ("span", "wrap"))),
        check_vma=False,
    )
```
